32 devices in a mesh: gx: 2 (over x), gy: 4 (over y, core), gz: 4 (over z).
Axes of the slice: x: 2, y: 2, z: 4, core: 2. Of those that a mesh axis runs over, the one named last changes fastest.
Arguments:
- panel: float32 [128, 131072], P(None, ('gx', 'gy', 'gz')), may hold values from -3000 to 3000
- trailing: float32 [64, 131072], P(None, ('gx', 'gy', 'gz')), may hold values from -6 to 6
Outputs:
- basis: float32 [128, 131072], P(None, ('gx', 'gy', 'gz'))
- upper: float32 [128, 128], replicated
- coupling: float32 [128, 64], replicated
- updated: float32 [64, 131072], P(None, ('gx', 'gy', 'gz'))
The draws below stay inside these ranges and needn't reach their ends.
All inputs are finite; a program needn't handle non-finite values.
Results may differ from the reference program's by a relative error of at most 0.0033.
Values sent between devices are 32-bit elements; how exact they have to be, the bound alone decides.
A program may use at most 64 MiB of HBM per device.

```python
import jax
import jax.numpy as jnp
from jax import lax

P_SIZE = 128
TRAIL = 64
ROWS = 131072


def draw_panel(key, part):
    k_base, k_cols, k_rows, k_left, k_right, k_sing = jax.random.split(jax.random.fold_in(key, 17), 6)
    left_turn, _ = jnp.linalg.qr(jax.random.normal(k_left, (P_SIZE, P_SIZE), jnp.float32))
    right_turn, _ = jnp.linalg.qr(jax.random.normal(k_right, (P_SIZE, P_SIZE), jnp.float32))
    spread = jnp.log(500.0)
    place = jnp.arange(P_SIZE, dtype=jnp.int32)
    base = jax.random.truncated_normal(k_base, -4.0, 4.0, (P_SIZE, ROWS), jnp.float32)
    cols = jnp.exp(jax.random.uniform(k_cols, (P_SIZE, 1), jnp.float32, 0.0, jnp.log(10.0)))
    level = jax.random.uniform(k_sing, (P_SIZE,), jnp.float32, 0.0, 1.0)
    level = jnp.where(place == 0, 0.0, jnp.where(place == 1, 1.0, level))
    singular = jnp.exp(-spread * level)
    mixing = jnp.dot(left_turn * singular[None, :], right_turn, precision=lax.Precision.HIGHEST)
    mixed = 3.5 * jnp.dot(mixing, base, precision=lax.Precision.HIGHEST)
    rising = 1.0 + 2.0 * jnp.arange(ROWS, dtype=jnp.float32)[None, :] / ROWS
    rows = jnp.exp(jax.random.uniform(k_rows, (1, ROWS), jnp.float32, 0.0, jnp.log(10.0))) * rising
    return jnp.clip(mixed * cols * rows, -3000.0, 3000.0)


def block_levels(stream_key, shape, cuts, low, high):
    def one(axis_at, blocks):
        draws = jax.random.uniform(jax.random.fold_in(jax.random.fold_in(stream_key, 6), axis_at), (blocks,), jnp.float32, low / len(cuts), high / len(cuts))
        return jnp.repeat(jnp.exp(draws), shape[axis_at] // blocks).reshape((-1,) + (1,) * (len(shape) - axis_at - 1))

    level = one(*cuts[0])
    for cut in cuts[1:]:
        level = level * one(*cut)
    return level


def normal_values(stream_key, dims, scale, limit, cuts=(), kind=jnp.bfloat16):
    array = scale * jax.random.normal(stream_key, dims, jnp.float32)
    if cuts:
        array = array * block_levels(stream_key, dims, cuts, -0.22, 0.18)
    return jnp.clip(array, -limit, limit).astype(kind)


def setup_inputs(seed: int = 0) -> dict:
    seeds = jax.random.split(jax.random.key(seed), 3)
    panel = draw_panel(jax.random.fold_in(seeds[2], 71), 0)
    trailing = normal_values(seeds[1], (TRAIL, ROWS), 1.0, 6.0, ((1, 32),), jnp.float32)
    return {"panel": panel, "trailing": trailing}


def matmul(left, right):
    return jnp.dot(left.astype(jnp.float32), right.astype(jnp.float32), precision=lax.Precision.HIGHEST, preferred_element_type=jnp.float32)

def lower_solve(lower, rhs):
    return lax.linalg.triangular_solve(lower, rhs, left_side=True, lower=True)

def reference(panel, trailing):
    first_low = jnp.linalg.cholesky(matmul(panel, panel.T))
    first = lower_solve(first_low, panel)
    second_low = jnp.linalg.cholesky(matmul(first, first.T))
    basis_t = lower_solve(second_low, first)
    whole_low = matmul(first_low, second_low)
    coupling = matmul(basis_t, trailing.T)
    updated = trailing - matmul(coupling.T, basis_t)
    scale = jnp.sqrt(jnp.float32(ROWS))
    return (basis_t * scale, whole_low.T / scale, coupling, updated)
```

```python
import functools

import jax
import jax.numpy as jnp
from jax import lax
from jax.experimental import pallas as pl
from jax.experimental.pallas import tpu as pltpu
from jax.sharding import PartitionSpec as P

MESH = pl.DeviceIdType.MESH
NT = (((1,), (1,)), ((), ()))
NN = (((1,), (0,)), ((), ()))
VMEM = pl.BlockSpec(memory_space=pltpu.VMEM)
HBM = pl.BlockSpec(memory_space=pltpu.HBM)


def dot(left, right, dims):
    return lax.dot_general(left, right, dims, preferred_element_type=jnp.float32)


def terms(value, count):
    found = []
    for _ in range(count):
        term = value.astype(jnp.bfloat16)
        found.append(term)
        value = value - term.astype(jnp.float32)
    return found


def left_terms(value):
    one, two, three = terms(value, 3)
    return jnp.concatenate([three, one, two, two, one, one], axis=1)


def right_terms(value, axis):
    one, two, three = terms(value, 3)
    return jnp.concatenate([one, three, two, one, two, one], axis=axis)


def product(left, right, dims):
    return dot(left_terms(left), right_terms(right, 1 if dims is NT else 0), dims)


def slices(value):
    top = jnp.max(jnp.abs(value), axis=1, keepdims=True) * 2.0**17
    high = (value + top) - top
    rest = value - high
    top = top * 2.0**-9
    middle = (rest + top) - top
    return high.astype(jnp.bfloat16), middle.astype(jnp.bfloat16), (rest - middle).astype(jnp.bfloat16)


def two_sum(one, two):
    total = one + two
    added = total - one
    return total, (one - (total - added)) + (two - added)


def factor(tiles):
    size = tiles[0].shape[1]
    lane = lax.broadcasted_iota(jnp.int32, (1, size), 1)
    row_in_tile = lax.broadcasted_iota(jnp.int32, (8, 1), 0)
    lanes = lax.broadcasted_iota(jnp.int32, (8, size), 1)
    tiles = list(tiles)
    for at in range(len(tiles)):
        first = 8 * at
        inside = (lane >= first) & (lane < first + 8)
        columns = {h: [jnp.broadcast_to(tiles[h][:, first + j : first + j + 1], (8, size)) for j in range(8)] for h in range(at, len(tiles))}
        for h in range(at + 1, len(tiles)):
            tiles[h] = jnp.where(inside, 0.0, tiles[h])
        for r in range(8):
            k = first + r
            row = tiles[at][r : r + 1, :]
            unit = jnp.where(lane == k, 1.0, row)
            behind = jnp.where(inside & (lane > k), 0.0, unit)
            pivots = [columns[at][j][r : r + 1, :] for j in range(8)]
            over = 1.0 / pivots[r]
            for h in range(at, len(tiles)):
                if h == at and r == 7:
                    continue
                times = columns[h][r] * over
                for j in range(r + 1, 8):
                    columns[h][j] = columns[h][j] - times * pivots[j]
                if h == at:
                    below = row_in_tile > r
                    tiles[h] = jnp.where(below, jnp.where(lanes == k, 0.0, tiles[h]) - times * unit, tiles[h])
                else:
                    tiles[h] = tiles[h] - times * behind
    uppers, inverses = [], []
    for h, tile in enumerate(tiles):
        rows = row_in_tile + 8 * h
        pivot = jnp.sum(jnp.where(lanes == rows, tile, 0.0), axis=1, keepdims=True)
        root = jnp.sqrt(pivot)
        over = 1.0 / root
        uppers.append(jnp.where(lanes > rows, tile * over, jnp.where(lanes == rows, root, 0.0)))
        inverses.append(jnp.where(lanes < rows, tile * over, jnp.where(lanes == rows, over, 0.0)))
    return uppers, inverses


def greet(sizes):
    nx, ny, nz = sizes
    gx, gy, gz = lax.axis_index("gx"), lax.axis_index("gy"), lax.axis_index("gz")
    barrier = pltpu.get_barrier_semaphore()
    me = gx * ny + gy
    for step in range(1, nx * ny):
        peer = lax.rem(me + step, nx * ny)
        pl.semaphore_signal(barrier, inc=1, device_id=(peer // ny, lax.rem(peer, ny), gz), device_id_type=MESH)
    for step in range(1, nz):
        pl.semaphore_signal(barrier, inc=1, device_id=(gx, gy, lax.rem(gz + step, nz)), device_id_type=MESH)


class Exchange:
    def __init__(self, sizes, send, landed, column, gathered, send_sem, recv_sem):
        nx, ny, nz = sizes
        self.nz, self.group = nz, nx * ny
        self.send, self.landed, self.column, self.gathered = send, landed, column, gathered
        gx, gy, gz = lax.axis_index("gx"), lax.axis_index("gy"), lax.axis_index("gz")
        group = self.group
        self.me, self.gz = gx * ny + gy, gz
        me = self.me

        def copy(src, dst, at, device):
            return pltpu.make_async_remote_copy(
                src_ref=src, dst_ref=dst, send_sem=send_sem.at[at], recv_sem=recv_sem.at[at], device_id=device, device_id_type=MESH
            )

        def in_plane(step):
            peer = lax.rem(me + step, group)
            return peer, (peer // ny, lax.rem(peer, ny), gz)

        self.out, self.back = [], []
        for step in range(1, group):
            peer, device = in_plane(step)
            self.out.append(copy(send.at[peer], landed.at[step], step, device))
            self.back.append(copy(gathered.at[me], gathered.at[me], group + nz + step, device))
        self.along = [
            copy(column.at[gz], column.at[gz], group + step, (gx, gy, lax.rem(gz + step, nz))) for step in range(1, nz)
        ]

    def parts(self):
        yield self.send[self.me]
        for step in range(1, self.group):
            self.out[step - 1].wait_recv()
            yield self.landed[step]

    def columns(self):
        for copy in self.along:
            copy.wait_recv()
        for z in range(self.nz):
            yield self.column[z]

    def finish(self):
        for copy in self.back:
            copy.wait_recv()

    def drain(self):
        for copy in self.out + self.along + self.back:
            copy.wait_send()


def start(copies):
    for copy in copies:
        copy.start()


def sum_pairs(values):
    total, lost = None, None
    for value in values:
        if total is None:
            total = value
        else:
            total, off = two_sum(total, value)
            lost = off if lost is None else lost + off
    return total, jnp.zeros_like(total) if lost is None else lost


def sum_plain(values):
    total = None
    for value in values:
        total = value if total is None else total + value
    return total


def exchange_scratch(sizes, rows, size):
    nx, ny, nz = sizes
    group = nx * ny
    return [
        pltpu.VMEM((group, rows, size), jnp.float32),
        pltpu.VMEM((group, rows, size), jnp.float32),
        pltpu.VMEM((nz, rows, size), jnp.float32),
        pltpu.VMEM((group, rows, size), jnp.float32),
        pltpu.SemaphoreType.DMA((2 * group + nz,)),
        pltpu.SemaphoreType.DMA((2 * group + nz,)),
    ]


def chunk_of(width, most):
    return most if width % most == 0 else width


def reduce_kernel(sizes, panel, trailing, gram_out, rest_out, upper_out, inverse_out, panel_held, trailing_held, sliced, move_sem, *scratch):
    size, width = panel.shape
    trail = trailing.shape[0]
    group = sizes[0] * sizes[1]
    rows, less = size // group, trail // group
    chunk = chunk_of(width, 1024)
    steps = width // chunk
    greet(sizes)
    loads, more = [], []
    for i in range(steps):
        at = pl.ds(i * chunk, chunk)
        loads.append(pltpu.make_async_copy(panel.at[:, at], panel_held.at[:, at], move_sem.at[0, i]))
        loads[-1].start()
    for i in range(steps):
        at = pl.ds(i * chunk, chunk)
        more.append(pltpu.make_async_copy(trailing.at[:, at], trailing_held.at[:, at], move_sem.at[1, i]))
        more[-1].start()
    zero = jnp.zeros((size, size), jnp.float32)
    gram, lost, mixed, small = zero, zero, zero, zero
    for i in range(steps):
        loads[i].wait()
        at = slice(i * chunk, (i + 1) * chunk)
        high, middle, low = slices(panel_held[:, at])
        pair = jnp.concatenate([high, middle], axis=0)
        sliced[: 2 * size, at] = pair
        sliced[2 * size :, at] = low
        first = dot(pair, pair, NT)
        second = dot(low, pair, NT)
        gram, off = two_sum(gram, first[:size, :size])
        lost = lost + off
        mixed = mixed + (first[:size, size:] + (second[:, :size] + second[:, size:]))
        small = small + (first[size:, size:] + dot(low, low, NT))
    gram, off = two_sum(gram, small + (mixed + mixed.T))
    lost = lost + off
    heads = Exchange(sizes, *scratch[:6])
    tails = Exchange(sizes, *scratch[6:])
    for p in range(group):
        heads.send[p] = gram[p * rows : (p + 1) * rows]
    pl.semaphore_wait(pltpu.get_barrier_semaphore(), group - 1 + sizes[2] - 1)
    start(heads.out)
    cross = jnp.zeros((trail, size), jnp.float32)
    for i in range(steps):
        more[i].wait()
        at = slice(i * chunk, (i + 1) * chunk)
        found = dot(jnp.concatenate(terms(trailing_held[:, at], 2), axis=0), sliced[:, at], NT)
        found = found[:trail] + found[trail:]
        cross = cross + (found[:, :size] + (found[:, size : 2 * size] + found[:, 2 * size :]))
    for p in range(group):
        tails.send[p, :rows] = lost[p * rows : (p + 1) * rows]
        tails.send[p, rows:] = cross[p * less : (p + 1) * less]
    start(tails.out)
    total, lost_out = sum_pairs(heads.parts())
    heads.column[heads.gz] = total
    start(heads.along)
    part = sum_plain(tails.parts())
    tails.column[tails.gz, :rows] = part[:rows] + lost_out
    tails.column[tails.gz, rows:] = part[rows:]
    total, lost_along = sum_pairs(heads.columns())
    heads.gathered[heads.me] = total
    start(heads.back)
    start(tails.along)
    part = sum_plain(tails.columns())
    tails.gathered[tails.me, :rows] = part[:rows] + lost_along
    tails.gathered[tails.me, rows:] = part[rows:]
    heads.finish()
    start(tails.back)
    gram = jnp.concatenate([heads.gathered[p] for p in range(group)], axis=0)
    uppers, inverses = factor([gram[h : h + 8] for h in range(0, size, 8)])
    for h in range(len(uppers)):
        upper_out[8 * h : 8 * h + 8] = uppers[h]
        inverse_out[8 * h : 8 * h + 8] = inverses[h]
    gram_out[...] = gram
    tails.finish()
    for p in range(group):
        rest_out[p] = tails.gathered[p]
    heads.drain()
    tails.drain()


def refine(gram, lost, cross, first_upper, inverse):
    size = gram.shape[0]
    row = lax.broadcasted_iota(jnp.int32, (size, size), 0)
    lane = lax.broadcasted_iota(jnp.int32, (size, size), 1)
    high, middle, low = slices(first_upper.T)
    pair = jnp.concatenate([high, middle], axis=0)
    first = dot(pair, pair, NT)
    second = dot(low, pair, NT)
    mixed = first[:size, size:] + (second[:, :size] + second[:, size:])
    small = (first[size:, size:] + dot(low, low, NT)) + (mixed + mixed.T)
    off, lower_off = two_sum(gram, -first[:size, :size])
    off = (off - small) + (lower_off + lost)
    lower = (high.astype(jnp.float32) + middle.astype(jnp.float32)) + low.astype(jnp.float32)
    both = product(inverse, jnp.concatenate([lower, off], axis=1), NN)
    second_gram = product(both, jnp.concatenate([both[:, :size], inverse], axis=1), NT)

    def correction(value):
        return jnp.where(row > lane, -value, jnp.where(row == lane, 1.5 - 0.5 * value, 0.0))

    step = correction(second_gram)
    inverse = product(step, inverse, NN)
    step = correction(product(product(step, second_gram, NN), step, NT))
    inverse = product(step, inverse, NN)
    mixed = product(cross, inverse, NT)
    upper = product(inverse, gram, NN) + product(inverse, lost, NN)
    return inverse, product(mixed, inverse, NN), jnp.where(row <= lane, upper, 0.0), mixed


def final_kernel(scale, gram, rest, first_upper, inverse, panel, trailing, basis, upper, coupling, updated, panel_held, trailing_held, basis_held, updated_held, upper_held, coupling_held, load_sem, store_sem):
    size, width = panel.shape
    trail = trailing.shape[0]
    chunk = chunk_of(width, 512)
    loads = [
        pltpu.make_async_copy(panel, panel_held, load_sem.at[0]),
        pltpu.make_async_copy(trailing, trailing_held, load_sem.at[1]),
    ]
    start(loads)
    group = rest.shape[0]
    rows = size // group
    lost = jnp.concatenate([rest[p, :rows] for p in range(group)], axis=0)
    cross = jnp.concatenate([rest[p, rows:] for p in range(group)], axis=0)
    whole, projected, total, mixed = refine(gram[...], lost, cross, first_upper[...], inverse[...])
    coupling_held[...] = mixed
    upper_held[...] = total * (1.0 / scale)
    stores = [
        pltpu.make_async_copy(coupling_held, coupling, load_sem.at[2]),
        pltpu.make_async_copy(upper_held, upper, load_sem.at[3]),
    ]
    start(stores)
    left = left_terms(jnp.concatenate([whole * scale, projected], axis=0))
    for load in loads:
        load.wait()
    for i in range(width // chunk):
        at = pl.ds(i * chunk, chunk)
        out = dot(left, right_terms(panel_held[:, at], 0), NN)
        basis_held[:, at] = out[:size]
        updated_held[:, at] = trailing_held[:, at] - out[size:]
        for place, (src, dst) in enumerate(((basis_held, basis), (updated_held, updated))):
            stores.append(pltpu.make_async_copy(src.at[:, at], dst.at[:, at], store_sem.at[place, i]))
            stores[-1].start()
    for store in stores:
        store.wait()


def shards(sizes, panel, trailing):
    size, width = panel.shape
    trail = trailing.shape[0]
    nx, ny, nz = sizes
    group = nx * ny
    rows, less = size // group, trail // group
    f32 = jnp.float32
    scale = float(width * group * nz) ** 0.5

    def params(identity=None, mebibytes=53):
        return pltpu.CompilerParams(
            collective_id=identity, has_side_effects=identity is not None, vmem_limit_bytes=mebibytes * 2**20
        )

    square = jax.ShapeDtypeStruct((size, size), f32)
    gram, rest, first_upper, inverse = pl.pallas_call(
        functools.partial(reduce_kernel, sizes),
        out_shape=[square, jax.ShapeDtypeStruct((group, rows + less, size), f32), square, square],
        in_specs=[HBM, HBM],
        out_specs=[VMEM] * 4,
        scratch_shapes=[
            pltpu.VMEM((size, width), f32),
            pltpu.VMEM((trail, width), f32),
            pltpu.VMEM((3 * size, width), jnp.bfloat16),
            pltpu.SemaphoreType.DMA((2, width // chunk_of(width, 1024))),
            *exchange_scratch(sizes, rows, size),
            *exchange_scratch(sizes, rows + less, size),
        ],
        compiler_params=params(0),
        name="reduce",
    )(panel, trailing)
    basis, upper, coupling_t, updated = pl.pallas_call(
        functools.partial(final_kernel, scale),
        out_shape=[
            jax.ShapeDtypeStruct((size, width), f32),
            square,
            jax.ShapeDtypeStruct((trail, size), f32),
            jax.ShapeDtypeStruct((trail, width), f32),
        ],
        in_specs=[VMEM] * 4 + [HBM] * 2,
        out_specs=[HBM] * 4,
        scratch_shapes=[
            pltpu.VMEM((size, width), f32),
            pltpu.VMEM((trail, width), f32),
            pltpu.VMEM((size, width), f32),
            pltpu.VMEM((trail, width), f32),
            pltpu.VMEM((size, size), f32),
            pltpu.VMEM((trail, size), f32),
            pltpu.SemaphoreType.DMA((4,)),
            pltpu.SemaphoreType.DMA((2, width // chunk_of(width, 512))),
        ],
        compiler_params=params(),
        name="final",
    )(gram, rest, first_upper, inverse, panel, trailing)
    return basis, upper, coupling_t.T, updated


def solution(mesh):
    sizes = tuple(mesh.shape[name] for name in ("gx", "gy", "gz"))
    placed = P(None, ("gx", "gy", "gz"))
    return jax.shard_map(
        functools.partial(shards, sizes),
        mesh=mesh,
        in_specs=(placed, placed),
        out_specs=(placed, P(), P(), placed),
        check_vma=False,
    )
```

```python
import functools

import jax
import jax.numpy as jnp
from jax import lax
from jax.experimental import pallas as pl
from jax.experimental.pallas import tpu as pltpu
from jax.sharding import PartitionSpec as P

MESH = pl.DeviceIdType.MESH
NT = (((1,), (1,)), ((), ()))
NN = (((1,), (0,)), ((), ()))
TN = (((0,), (0,)), ((), ()))
VMEM = pl.BlockSpec(memory_space=pltpu.VMEM)
HBM = pl.BlockSpec(memory_space=pltpu.HBM)


def dot(left, right, dims):
    return lax.dot_general(left, right, dims, preferred_element_type=jnp.float32)


def terms(value, count):
    found = []
    for _ in range(count):
        term = value.astype(jnp.bfloat16)
        found.append(term)
        value = value - term.astype(jnp.float32)
    return found


def left_terms(value):
    one, two, three = terms(value, 3)
    return jnp.concatenate([three, one, two, two, one, one], axis=1)


def right_terms(value, axis):
    one, two, three = terms(value, 3)
    return jnp.concatenate([one, three, two, one, two, one], axis=axis)


def product(left, right, dims):
    return dot(left_terms(left), right_terms(right, 1 if dims is NT else 0), dims)


def slices(value):
    top = jnp.max(jnp.abs(value), axis=1, keepdims=True) * 2.0**17
    high = (value + top) - top
    rest = value - high
    top = top * 2.0**-9
    middle = (rest + top) - top
    return high.astype(jnp.bfloat16), middle.astype(jnp.bfloat16), (rest - middle).astype(jnp.bfloat16)


def two_sum(one, two):
    total = one + two
    added = total - one
    return total, (one - (total - added)) + (two - added)


def factor(tiles, depth=8):
    size = tiles[0].shape[1]
    shape = (8, size)
    lanes = lax.broadcasted_iota(jnp.int32, shape, 1)
    row_in_tile = lax.broadcasted_iota(jnp.int32, shape, 0)
    tiles = list(tiles)
    count = len(tiles)

    def across(tile, column):
        return jnp.broadcast_to(jnp.sum(jnp.where(lanes == column, tile, 0.0), axis=1, keepdims=True), shape)

    def down(tile, row):
        return jnp.broadcast_to(tile[row : row + 1, :], shape)

    for start in range(0, count, depth):
        stop = min(start + depth, count)
        own = [across(tiles[start], 8 * start + j) for j in range(8)]
        scales = []
        for at in range(start, stop):
            first = 8 * at
            inside = (lanes >= first) & (lanes < first + 8)
            raw = list(tiles)
            columns = after = None
            if at + 1 < stop:
                columns = [across(raw[at + 1], first + j) for j in range(8)]
                after = [across(raw[at + 1], first + 8 + j) for j in range(8)]
            tile = tiles[at]
            scaled, ratios, scale = [], [], None
            for h in range(at + 1, stop):
                tiles[h] = jnp.where(inside, 0.0, tiles[h])
            for r in range(8):
                k = first + r
                pivots = {j: down(own[j], r) for j in range(r, 8)}
                over = 1.0 / pivots[r]
                scale = over if scale is None else jnp.where(row_in_tile == r, over, scale)
                ratios.append({j: pivots[j] * over for j in range(r + 1, 8)})
                unit = jnp.where(lanes == k, 1.0, down(tile, r))
                scaled.append(jnp.where(inside & (lanes > k), 0.0, unit) * over)
                if r < 7:
                    for j in range(r + 1, 8):
                        own[j] = own[j] - own[r] * ratios[r][j]
                    below = jnp.where(lanes == k, 0.0, tile) - (own[r] * over) * unit
                    tile = jnp.where(row_in_tile > r, below, tile)
                if after is not None:
                    column = columns[r]
                    for j in range(r + 1, 8):
                        columns[j] = columns[j] - column * ratios[r][j]
                    tiles[at + 1] = tiles[at + 1] - column * scaled[r]
                    times = column * over
                    for j in range(8):
                        after[j] = after[j] - times * down(column, j)
            tiles[at] = tile
            scales.append(scale)
            for h in range(at + 2, stop):
                columns = [across(raw[h], first + j) for j in range(8)]
                total = tiles[h]
                for r in range(8):
                    column = columns[r]
                    for j in range(r + 1, 8):
                        columns[j] = columns[j] - column * ratios[r][j]
                    total = total - column * scaled[r]
                tiles[h] = total
            own = after
        if stop < count:
            inner = (lanes >= 8 * start) & (lanes < 8 * stop)
            left = jnp.concatenate(tiles[start:stop], axis=0)
            right = []
            for h in range(start, stop):
                rows = row_in_tile + 8 * h
                right.append(jnp.where(lanes == rows, 1.0, jnp.where(inner & (lanes > rows), 0.0, tiles[h])) * scales[h - start])
            b1, b2, b3 = terms(jnp.concatenate(right, axis=0), 3)
            a1, a2, a3 = terms(left, 3)
            a = jnp.concatenate([a3, a1, a2, a2, a1, a1], axis=0)
            update = dot(a, jnp.concatenate([b1, b3, b2, b1, b2, b1], axis=0), TN)
            for h in range(stop, count):
                tiles[h] = jnp.where(inner, 0.0, tiles[h]) - update[8 * h : 8 * h + 8]
    uppers, inverses = [], []
    for h, tile in enumerate(tiles):
        rows = row_in_tile + 8 * h
        pivot = jnp.sum(jnp.where(lanes == rows, tile, 0.0), axis=1, keepdims=True)
        root = jnp.sqrt(pivot)
        over = 1.0 / root
        uppers.append(jnp.where(lanes > rows, tile * over, jnp.where(lanes == rows, root, 0.0)))
        inverses.append(jnp.where(lanes < rows, tile * over, jnp.where(lanes == rows, over, 0.0)))
    return uppers, inverses


def greet(sizes):
    nx, ny, nz = sizes
    gx, gy, gz = lax.axis_index("gx"), lax.axis_index("gy"), lax.axis_index("gz")
    barrier = pltpu.get_barrier_semaphore()
    me = gx * ny + gy
    for step in range(1, nx * ny):
        peer = lax.rem(me + step, nx * ny)
        pl.semaphore_signal(barrier, inc=1, device_id=(peer // ny, lax.rem(peer, ny), gz), device_id_type=MESH)
    for step in range(1, nz):
        pl.semaphore_signal(barrier, inc=1, device_id=(gx, gy, lax.rem(gz + step, nz)), device_id_type=MESH)


class Exchange:
    def __init__(self, sizes, send, landed, column, gathered, send_sem, recv_sem):
        nx, ny, nz = sizes
        self.nz, self.group = nz, nx * ny
        self.send, self.landed, self.column, self.gathered = send, landed, column, gathered
        gx, gy, gz = lax.axis_index("gx"), lax.axis_index("gy"), lax.axis_index("gz")
        group = self.group
        self.me, self.gz = gx * ny + gy, gz
        me = self.me

        def copy(src, dst, at, device):
            return pltpu.make_async_remote_copy(
                src_ref=src, dst_ref=dst, send_sem=send_sem.at[at], recv_sem=recv_sem.at[at], device_id=device, device_id_type=MESH
            )

        def in_plane(step):
            peer = lax.rem(me + step, group)
            return peer, (peer // ny, lax.rem(peer, ny), gz)

        self.out, self.back = [], []
        for step in range(1, group):
            peer, device = in_plane(step)
            self.out.append(copy(send.at[peer], landed.at[step], step, device))
            self.back.append(copy(gathered.at[me], gathered.at[me], group + nz + step, device))
        self.along = [
            copy(column.at[gz], column.at[gz], group + step, (gx, gy, lax.rem(gz + step, nz))) for step in range(1, nz)
        ]

    def parts(self):
        yield self.send[self.me]
        for step in range(1, self.group):
            self.out[step - 1].wait_recv()
            yield self.landed[step]

    def columns(self):
        for copy in self.along:
            copy.wait_recv()
        for z in range(self.nz):
            yield self.column[z]

    def finish(self):
        for copy in self.back:
            copy.wait_recv()

    def drain(self):
        for copy in self.out + self.along + self.back:
            copy.wait_send()


def start(copies):
    for copy in copies:
        copy.start()


def sum_pairs(values):
    total, lost = None, None
    for value in values:
        if total is None:
            total = value
        else:
            total, off = two_sum(total, value)
            lost = off if lost is None else lost + off
    return total, jnp.zeros_like(total) if lost is None else lost


def sum_plain(values):
    total = None
    for value in values:
        total = value if total is None else total + value
    return total


def exchange_scratch(sizes, rows, size):
    nx, ny, nz = sizes
    group = nx * ny
    return [
        pltpu.VMEM((group, rows, size), jnp.float32),
        pltpu.VMEM((group, rows, size), jnp.float32),
        pltpu.VMEM((nz, rows, size), jnp.float32),
        pltpu.VMEM((group, rows, size), jnp.float32),
        pltpu.SemaphoreType.DMA((2 * group + nz,)),
        pltpu.SemaphoreType.DMA((2 * group + nz,)),
    ]


def chunk_of(width, most):
    return most if width % most == 0 else width


def reduce_kernel(sizes, panel, trailing, gram_out, rest_out, off_out, product_out, inverse_out, pieces, trailing_held, panel_held, sliced, move_sem, *scratch):
    size, width = panel.shape
    trail = trailing.shape[0]
    group = sizes[0] * sizes[1]
    rows, less = size // group, trail // group
    chunk = chunk_of(width, 512)
    steps = width // chunk
    spans = [slice(i * chunk, (i + 1) * chunk) for i in range(steps)]
    loads = []
    for i in range(steps):
        at = pl.ds(i * chunk, chunk)
        loads.append(pltpu.make_async_copy(panel.at[:, at], panel_held.at[:, at], move_sem.at[i]))
    loads.append(pltpu.make_async_copy(trailing, trailing_held, move_sem.at[steps]))
    start(loads)
    greet(sizes)
    zero = jnp.zeros((size, size), jnp.float32)
    gram, lost, mixed, small = zero, zero, zero, zero
    for i in range(steps + 1):
        if i < steps:
            loads[i].wait()
            high, middle, low = slices(panel_held[:, spans[i]])
            sliced[:size, spans[i]] = high
            sliced[size : 2 * size, spans[i]] = middle
            sliced[2 * size :, spans[i]] = low
        if i > 0:
            pair = sliced[: 2 * size, spans[i - 1]]
            first = dot(pair, pair, NT)
            second = dot(sliced[2 * size :, spans[i - 1]], pair, NT)
            gram, off = two_sum(gram, first[:size, :size])
            lost = lost + off
            mixed = mixed + (first[:size, size:] + (second[:, :size] + second[:, size:]))
            small = small + first[size:, size:]
    gram, off = two_sum(gram, small + (mixed + mixed.T))
    lost = lost + off
    heads = Exchange(sizes, *scratch[:6])
    tails = Exchange(sizes, *scratch[6:])
    for p in range(group):
        heads.send[p] = gram[p * rows : (p + 1) * rows]
    pl.semaphore_wait(pltpu.get_barrier_semaphore(), group - 1 + sizes[2] - 1)
    start(heads.out)
    loads[steps].wait()
    cross = jnp.zeros((trail, size), jnp.float32)
    for span in spans:
        both = jnp.concatenate(terms(trailing_held[:, span], 2), axis=0)
        low = sliced[2 * size :, span]
        found = dot(both, sliced[: 2 * size, span], NT)
        last = dot(jnp.concatenate([low, both], axis=0), low, NT)
        found = found[:, :size] + (found[:, size:] + last[size:])
        cross = cross + (found[:trail] + found[trail:])
        lost = lost + last[:size]
    for p in range(group):
        tails.send[p, :rows] = lost[p * rows : (p + 1) * rows]
        tails.send[p, rows:] = cross[p * less : (p + 1) * less]
    total, lost_out = sum_pairs(heads.parts())
    heads.column[heads.gz] = total
    start(heads.along)
    start(tails.out)
    for span in spans[: steps // 2]:
        for t, term in enumerate(terms(panel_held[:, span], 3)):
            pieces[t * size : (t + 1) * size, span] = term
    total, lost_along = sum_pairs(heads.columns())
    heads.gathered[heads.me] = total
    start(heads.back)
    part = sum_plain(tails.parts())
    tails.column[tails.gz, :rows] = part[:rows] + lost_out
    tails.column[tails.gz, rows:] = part[rows:]
    start(tails.along)
    for span in spans[steps // 2 :]:
        for t, term in enumerate(terms(panel_held[:, span], 3)):
            pieces[t * size : (t + 1) * size, span] = term
    heads.finish()
    part = sum_plain(tails.columns())
    tails.gathered[tails.me, :rows] = part[:rows] + lost_along
    tails.gathered[tails.me, rows:] = part[rows:]
    start(tails.back)
    gram = jnp.concatenate([heads.gathered[p] for p in range(group)], axis=0)
    uppers, inverses = factor([gram[h : h + 8] for h in range(0, size, 8)])
    inverse = jnp.concatenate(inverses, axis=0)
    gram_out[...] = gram
    inverse_out[...] = inverse
    off, turned = departure(gram, jnp.concatenate(uppers, axis=0), inverse)
    off_out[...] = off
    product_out[...] = turned
    tails.finish()
    for p in range(group):
        rest_out[p] = tails.gathered[p]
    heads.drain()
    tails.drain()


def departure(gram, upper, inverse):
    size = gram.shape[0]
    high, middle, low = slices(upper.T)
    pair = jnp.concatenate([high, middle], axis=0)
    first = dot(pair, pair, NT)
    second = dot(low, pair, NT)
    mixed = first[:size, size:] + (second[:, :size] + second[:, size:])
    small = (first[size:, size:] + dot(low, low, NT)) + (mixed + mixed.T)
    off, lower_off = two_sum(gram, -first[:size, :size])
    lower = (high.astype(jnp.float32) + middle.astype(jnp.float32)) + low.astype(jnp.float32)
    return (off - small) + lower_off, product(inverse, lower, NN)


def refine(off, turned, inverse):
    size = off.shape[0]
    row = lax.broadcasted_iota(jnp.int32, (size, size), 0)
    lane = lax.broadcasted_iota(jnp.int32, (size, size), 1)

    def correction(value):
        return jnp.where(row > lane, -value, jnp.where(row == lane, 1.5 - 0.5 * value, 0.0))

    moved = product(inverse, off, NN)
    second_gram = product(jnp.concatenate([turned, moved], axis=1), jnp.concatenate([turned, inverse], axis=1), NT)
    step = correction(second_gram)
    inverse = product(step, inverse, NN)
    step = correction(product(product(step, second_gram, NN), step, NT))
    return product(step, inverse, NN)


def final_kernel(scale, gram, rest, off, turned, inverse, pieces, trailing, basis, upper, coupling, updated, basis_held, updated_held, upper_held, coupling_held, store_sem):
    size, width = basis.shape
    chunk = chunk_of(width, 512)
    steps = width // chunk
    group = rest.shape[0]
    rows = size // group
    lost = jnp.concatenate([rest[p, :rows] for p in range(group)], axis=0)
    cross = jnp.concatenate([rest[p, rows:] for p in range(group)], axis=0)
    whole = refine(off[...] + lost, turned[...], inverse[...])
    left = left_terms(whole * scale)
    mixed = product(cross, whole, NT)
    coupling_held[...] = mixed
    one, two = terms(mixed * (1.0 / scale), 2)
    back = jnp.concatenate([two, one, one], axis=1)
    stores = []

    def store(src, dst, place):
        stores.append(pltpu.make_async_copy(src, dst, store_sem.at[place]))
        stores[-1].start()

    for i in range(steps):
        span, at = slice(i * chunk, (i + 1) * chunk), pl.ds(i * chunk, chunk)
        one, two, three = (pieces[t * size : (t + 1) * size, span] for t in range(3))
        out = dot(left, jnp.concatenate([one, three, two, one, two, one], axis=0), NN)
        basis_held[:, span] = out
        store(basis_held.at[:, at], basis.at[:, at], 2 * i)
        one, two = terms(out, 2)
        updated_held[:, span] = trailing[:, span] - dot(back, jnp.concatenate([one, two, one], axis=0), NN)
        store(updated_held.at[:, at], updated.at[:, at], 2 * i + 1)
        if i == 0:
            row = lax.broadcasted_iota(jnp.int32, (size, size), 0)
            lane = lax.broadcasted_iota(jnp.int32, (size, size), 1)
            total = product(whole, gram[...], NN) + product(whole, lost, NN)
            upper_held[...] = jnp.where(row <= lane, total * (1.0 / scale), 0.0)
            store(coupling_held, coupling, 2 * steps)
            store(upper_held, upper, 2 * steps + 1)
    for copy in stores:
        copy.wait()


def shards(sizes, panel, trailing):
    size, width = panel.shape
    trail = trailing.shape[0]
    nx, ny, nz = sizes
    group = nx * ny
    rows, less = size // group, trail // group
    f32 = jnp.float32
    scale = float(width * group * nz) ** 0.5

    def params(identity=None, mebibytes=40):
        return pltpu.CompilerParams(
            collective_id=identity, has_side_effects=identity is not None, vmem_limit_bytes=mebibytes * 2**20
        )

    square = jax.ShapeDtypeStruct((size, size), f32)
    held = pl.pallas_call(
        functools.partial(reduce_kernel, sizes),
        out_shape=[
            square,
            jax.ShapeDtypeStruct((group, rows + less, size), f32),
            square,
            square,
            square,
            jax.ShapeDtypeStruct((3 * size, width), jnp.bfloat16),
            jax.ShapeDtypeStruct((trail, width), f32),
        ],
        in_specs=[HBM, HBM],
        out_specs=[VMEM] * 7,
        scratch_shapes=[
            pltpu.VMEM((size, width), f32),
            pltpu.VMEM((3 * size, width), jnp.bfloat16),
            pltpu.SemaphoreType.DMA((width // chunk_of(width, 512) + 1,)),
            *exchange_scratch(sizes, rows, size),
            *exchange_scratch(sizes, rows + less, size),
        ],
        compiler_params=params(0),
        name="reduce",
    )(pltpu.with_memory_space_constraint(panel, pltpu.HBM), pltpu.with_memory_space_constraint(trailing, pltpu.HBM))
    basis, upper, coupling_t, updated = pl.pallas_call(
        functools.partial(final_kernel, scale),
        out_shape=[
            jax.ShapeDtypeStruct((size, width), f32),
            square,
            jax.ShapeDtypeStruct((trail, size), f32),
            jax.ShapeDtypeStruct((trail, width), f32),
        ],
        in_specs=[VMEM] * 7,
        out_specs=[HBM] * 4,
        scratch_shapes=[
            pltpu.VMEM((size, width), f32),
            pltpu.VMEM((trail, width), f32),
            pltpu.VMEM((size, size), f32),
            pltpu.VMEM((trail, size), f32),
            pltpu.SemaphoreType.DMA((2 * (width // chunk_of(width, 512)) + 2,)),
        ],
        compiler_params=params(),
        name="final",
    )(*held)
    return basis, upper, coupling_t.T, updated


def solution(mesh):
    sizes = tuple(mesh.shape[name] for name in ("gx", "gy", "gz"))
    placed = P(None, ("gx", "gy", "gz"))
    return jax.shard_map(
        functools.partial(shards, sizes),
        mesh=mesh,
        in_specs=(placed, placed),
        out_specs=(placed, P(), P(), placed),
        check_vma=False,
    )
```

```python
import functools

import jax
import jax.numpy as jnp
from jax import lax
from jax.experimental import pallas as pl
from jax.experimental.pallas import tpu as pltpu
from jax.sharding import PartitionSpec as P

MESH = pl.DeviceIdType.MESH
NT = (((1,), (1,)), ((), ()))
NN = (((1,), (0,)), ((), ()))
TN = (((0,), (0,)), ((), ()))
VMEM = pl.BlockSpec(memory_space=pltpu.VMEM)
HBM = pl.BlockSpec(memory_space=pltpu.HBM)


def dot(left, right, dims):
    return lax.dot_general(left, right, dims, preferred_element_type=jnp.float32)


def terms(value, count):
    found = []
    for _ in range(count):
        term = value.astype(jnp.bfloat16)
        found.append(term)
        value = value - term.astype(jnp.float32)
    return found


def left_terms(value):
    one, two, three = terms(value, 3)
    return jnp.concatenate([three, one, two, two, one, one], axis=1)


def right_terms(value, axis):
    one, two, three = terms(value, 3)
    return jnp.concatenate([one, three, two, one, two, one], axis=axis)


def product(left, right, dims):
    return dot(left_terms(left), right_terms(right, 1 if dims is NT else 0), dims)


def slices(value):
    top = jnp.max(jnp.abs(value), axis=1, keepdims=True) * 2.0**17
    high = (value + top) - top
    rest = value - high
    top = top * 2.0**-9
    middle = (rest + top) - top
    return high.astype(jnp.bfloat16), middle.astype(jnp.bfloat16), (rest - middle).astype(jnp.bfloat16)


def two_sum(one, two):
    total = one + two
    added = total - one
    return total, (one - (total - added)) + (two - added)


def factor(tiles, depth=8):
    size = tiles[0].shape[1]
    shape = (8, size)
    lanes = lax.broadcasted_iota(jnp.int32, shape, 1)
    row_in_tile = lax.broadcasted_iota(jnp.int32, shape, 0)
    tiles = list(tiles)
    count = len(tiles)

    def across(tile, column):
        return jnp.broadcast_to(jnp.sum(jnp.where(lanes == column, tile, 0.0), axis=1, keepdims=True), shape)

    def down(tile, row):
        return jnp.broadcast_to(tile[row : row + 1, :], shape)

    for start in range(0, count, depth):
        stop = min(start + depth, count)
        own = [across(tiles[start], 8 * start + j) for j in range(8)]
        scales = []
        for at in range(start, stop):
            first = 8 * at
            inside = (lanes >= first) & (lanes < first + 8)
            raw = list(tiles)
            columns = after = None
            if at + 1 < stop:
                columns = [across(raw[at + 1], first + j) for j in range(8)]
                after = [across(raw[at + 1], first + 8 + j) for j in range(8)]
            tile = tiles[at]
            scaled, ratios, scale = [], [], None
            for h in range(at + 1, stop):
                tiles[h] = jnp.where(inside, 0.0, tiles[h])
            for r in range(8):
                k = first + r
                pivots = {j: down(own[j], r) for j in range(r, 8)}
                over = 1.0 / pivots[r]
                scale = over if scale is None else jnp.where(row_in_tile == r, over, scale)
                ratios.append({j: pivots[j] * over for j in range(r + 1, 8)})
                unit = jnp.where(lanes == k, 1.0, down(tile, r))
                scaled.append(jnp.where(inside & (lanes > k), 0.0, unit) * over)
                if r < 7:
                    for j in range(r + 1, 8):
                        own[j] = own[j] - own[r] * ratios[r][j]
                    below = jnp.where(lanes == k, 0.0, tile) - (own[r] * over) * unit
                    tile = jnp.where(row_in_tile > r, below, tile)
                if after is not None:
                    column = columns[r]
                    for j in range(r + 1, 8):
                        columns[j] = columns[j] - column * ratios[r][j]
                    tiles[at + 1] = tiles[at + 1] - column * scaled[r]
                    times = column * over
                    for j in range(8):
                        after[j] = after[j] - times * down(column, j)
            tiles[at] = tile
            scales.append(scale)
            for h in range(at + 2, stop):
                columns = [across(raw[h], first + j) for j in range(8)]
                total = tiles[h]
                for r in range(8):
                    column = columns[r]
                    for j in range(r + 1, 8):
                        columns[j] = columns[j] - column * ratios[r][j]
                    total = total - column * scaled[r]
                tiles[h] = total
            own = after
        if stop < count:
            inner = (lanes >= 8 * start) & (lanes < 8 * stop)
            left = jnp.concatenate(tiles[start:stop], axis=0)
            right = []
            for h in range(start, stop):
                rows = row_in_tile + 8 * h
                right.append(jnp.where(lanes == rows, 1.0, jnp.where(inner & (lanes > rows), 0.0, tiles[h])) * scales[h - start])
            b1, b2, b3 = terms(jnp.concatenate(right, axis=0), 3)
            a1, a2, a3 = terms(left, 3)
            a = jnp.concatenate([a3, a1, a2, a2, a1, a1], axis=0)
            update = dot(a, jnp.concatenate([b1, b3, b2, b1, b2, b1], axis=0), TN)
            for h in range(stop, count):
                tiles[h] = jnp.where(inner, 0.0, tiles[h]) - update[8 * h : 8 * h + 8]
    uppers, inverses = [], []
    for h, tile in enumerate(tiles):
        rows = row_in_tile + 8 * h
        pivot = jnp.sum(jnp.where(lanes == rows, tile, 0.0), axis=1, keepdims=True)
        root = jnp.sqrt(pivot)
        over = 1.0 / root
        uppers.append(jnp.where(lanes > rows, tile * over, jnp.where(lanes == rows, root, 0.0)))
        inverses.append(jnp.where(lanes < rows, tile * over, jnp.where(lanes == rows, over, 0.0)))
    return uppers, inverses


def greet(sizes):
    nx, ny, nz = sizes
    gx, gy, gz = lax.axis_index("gx"), lax.axis_index("gy"), lax.axis_index("gz")
    barrier = pltpu.get_barrier_semaphore()
    me = gx * ny + gy
    for step in range(1, nx * ny):
        peer = lax.rem(me + step, nx * ny)
        pl.semaphore_signal(barrier, inc=1, device_id=(peer // ny, lax.rem(peer, ny), gz), device_id_type=MESH)
    for step in range(1, nz):
        pl.semaphore_signal(barrier, inc=1, device_id=(gx, gy, lax.rem(gz + step, nz)), device_id_type=MESH)


class Exchange:
    def __init__(self, sizes, send, landed, column, gathered, send_sem, recv_sem):
        nx, ny, nz = sizes
        self.nz, self.group = nz, nx * ny
        self.send, self.landed, self.column, self.gathered = send, landed, column, gathered
        gx, gy, gz = lax.axis_index("gx"), lax.axis_index("gy"), lax.axis_index("gz")
        group = self.group
        self.me, self.gz = gx * ny + gy, gz
        me = self.me

        def copy(src, dst, at, device):
            return pltpu.make_async_remote_copy(
                src_ref=src, dst_ref=dst, send_sem=send_sem.at[at], recv_sem=recv_sem.at[at], device_id=device, device_id_type=MESH
            )

        def in_plane(step):
            peer = lax.rem(me + step, group)
            return peer, (peer // ny, lax.rem(peer, ny), gz)

        self.out, self.back = [], []
        for step in range(1, group):
            peer, device = in_plane(step)
            self.out.append(copy(send.at[peer], landed.at[step], step, device))
            self.back.append(copy(gathered.at[me], gathered.at[me], group + nz + step, device))
        self.along = [
            copy(column.at[gz], column.at[gz], group + step, (gx, gy, lax.rem(gz + step, nz))) for step in range(1, nz)
        ]

    def parts(self):
        yield self.send[self.me]
        for step in range(1, self.group):
            self.out[step - 1].wait_recv()
            yield self.landed[step]

    def columns(self):
        for copy in self.along:
            copy.wait_recv()
        for z in range(self.nz):
            yield self.column[z]

    def finish(self):
        for copy in self.back:
            copy.wait_recv()

    def drain(self):
        for copy in self.out + self.along + self.back:
            copy.wait_send()


def start(copies):
    for copy in copies:
        copy.start()


def sum_pairs(values):
    total, lost = None, None
    for value in values:
        if total is None:
            total = value
        else:
            total, off = two_sum(total, value)
            lost = off if lost is None else lost + off
    return total, jnp.zeros_like(total) if lost is None else lost


def sum_plain(values):
    total = None
    for value in values:
        total = value if total is None else total + value
    return total


def exchange_scratch(sizes, rows, size):
    nx, ny, nz = sizes
    group = nx * ny
    return [
        pltpu.VMEM((group, rows, size), jnp.float32),
        pltpu.VMEM((group, rows, size), jnp.float32),
        pltpu.VMEM((nz, rows, size), jnp.float32),
        pltpu.VMEM((group, rows, size), jnp.float32),
        pltpu.SemaphoreType.DMA((2 * group + nz,)),
        pltpu.SemaphoreType.DMA((2 * group + nz,)),
    ]


def halves(span):
    middle = (span.start + span.stop) // 2
    return slice(span.start, middle), slice(middle, span.stop)


def chunk_of(width, most):
    return most if width % most == 0 else width


def reduce_kernel(sizes, panel, trailing, gram_out, rest_out, off_out, product_out, inverse_out, pieces, trailing_held, panel_held, sliced, move_sem, *scratch):
    size, width = panel.shape
    trail = trailing.shape[0]
    group = sizes[0] * sizes[1]
    rows, less = size // group, trail // group
    chunk = chunk_of(width, 1024)
    steps = width // chunk
    spans = [slice(i * chunk, (i + 1) * chunk) for i in range(steps)]
    loads = []
    for i in range(steps):
        at = pl.ds(i * chunk, chunk)
        loads.append(pltpu.make_async_copy(panel.at[:, at], panel_held.at[:, at], move_sem.at[i]))
    loads.append(pltpu.make_async_copy(trailing, trailing_held, move_sem.at[steps]))
    start(loads)
    greet(sizes)
    zero = jnp.zeros((size, size), jnp.float32)
    gram, lost, mixed, small = zero, zero, zero, zero
    for i in range(steps + 1):
        if i < steps:
            loads[i].wait()
            for t in range(0, size, 16):
                for place, part in enumerate(slices(panel_held[t : t + 16, spans[i]])):
                    sliced[place * size + t : place * size + t + 16, spans[i]] = part
        if i > 0:
            for half in halves(spans[i - 1]):
                found = dot(sliced[:, half], sliced[: 2 * size, half], NT)
                gram, off = two_sum(gram, found[:size, :size])
                lost = lost + off
                mixed = mixed + (found[:size, size:] + (found[2 * size :, :size] + found[2 * size :, size:]))
                small = small + found[size : 2 * size, size:]
    gram, off = two_sum(gram, small + (mixed + mixed.T))
    lost = lost + off
    heads = Exchange(sizes, *scratch[:6])
    tails = Exchange(sizes, *scratch[6:])
    for p in range(group):
        heads.send[p] = gram[p * rows : (p + 1) * rows]
    pl.semaphore_wait(pltpu.get_barrier_semaphore(), group - 1 + sizes[2] - 1)
    start(heads.out)
    loads[steps].wait()
    cross = jnp.zeros((trail, size), jnp.float32)
    for span in spans:
        both = jnp.concatenate(terms(trailing_held[:, span], 2), axis=0)
        low = sliced[2 * size :, span]
        found = dot(both, sliced[: 2 * size, span], NT)
        last = dot(jnp.concatenate([low, both], axis=0), low, NT)
        found = found[:, :size] + (found[:, size:] + last[size:])
        cross = cross + (found[:trail] + found[trail:])
        lost = lost + last[:size]
    for p in range(group):
        tails.send[p, :rows] = lost[p * rows : (p + 1) * rows]
        tails.send[p, rows:] = cross[p * less : (p + 1) * less]
    start(tails.out)
    for span in spans:
        for t in range(0, size, 16):
            for place, term in enumerate(terms(panel_held[t : t + 16, span], 3)):
                pieces[place * size + t : place * size + t + 16, span] = term
    total, lost_out = sum_pairs(heads.parts())
    heads.column[heads.gz] = total
    start(heads.along)
    part = sum_plain(tails.parts())
    tails.column[tails.gz, :rows] = part[:rows] + lost_out
    tails.column[tails.gz, rows:] = part[rows:]
    start(tails.along)
    total, lost_along = sum_pairs(heads.columns())
    heads.gathered[heads.me] = total
    start(heads.back)
    part = sum_plain(tails.columns())
    tails.gathered[tails.me, :rows] = part[:rows] + lost_along
    tails.gathered[tails.me, rows:] = part[rows:]
    start(tails.back)
    heads.finish()
    gram = jnp.concatenate([heads.gathered[p] for p in range(group)], axis=0)
    uppers, inverses = factor([gram[h : h + 8] for h in range(0, size, 8)])
    inverse = jnp.concatenate(inverses, axis=0)
    gram_out[...] = gram
    inverse_out[...] = inverse
    off, turned = departure(gram, jnp.concatenate(uppers, axis=0), inverse)
    off_out[...] = off
    product_out[...] = turned
    tails.finish()
    for p in range(group):
        rest_out[p] = tails.gathered[p]
    heads.drain()
    tails.drain()


def departure(gram, upper, inverse):
    size = gram.shape[0]
    high, middle, low = slices(upper.T)
    pair = jnp.concatenate([high, middle], axis=0)
    first = dot(pair, pair, NT)
    second = dot(low, pair, NT)
    mixed = first[:size, size:] + (second[:, :size] + second[:, size:])
    small = (first[size:, size:] + dot(low, low, NT)) + (mixed + mixed.T)
    off, lower_off = two_sum(gram, -first[:size, :size])
    lower = (high.astype(jnp.float32) + middle.astype(jnp.float32)) + low.astype(jnp.float32)
    return (off - small) + lower_off, product(inverse, lower, NN)


def refine(off, turned, inverse):
    size = off.shape[0]
    row = lax.broadcasted_iota(jnp.int32, (size, size), 0)
    lane = lax.broadcasted_iota(jnp.int32, (size, size), 1)

    moved = product(inverse, off, NN)
    second_gram = product(jnp.concatenate([turned, moved], axis=1), jnp.concatenate([turned, inverse], axis=1), NT)
    step = jnp.where(row > lane, second_gram, jnp.where(row == lane, 0.5 * second_gram - 0.5, 0.0))
    twice = product(step, jnp.concatenate([step, step.T], axis=1), NN)
    below = jnp.where(row > lane, twice[:, size:], jnp.where(row == lane, 0.5 * twice[:, size:], 0.0))
    return inverse + product((twice[:, :size] + below) - step, inverse, NN)


def final_kernel(scale, gram, rest, off, turned, inverse, pieces, trailing, basis, upper, coupling, updated, basis_held, updated_held, upper_held, coupling_held, store_sem):
    size, width = basis.shape
    chunk = chunk_of(width, 512)
    steps = width // chunk
    group = rest.shape[0]
    rows = size // group
    lost = jnp.concatenate([rest[p, :rows] for p in range(group)], axis=0)
    cross = jnp.concatenate([rest[p, rows:] for p in range(group)], axis=0)
    whole = refine(off[...] + lost, turned[...], inverse[...])
    mixed = product(cross, whole, NT)
    coupling_held[...] = mixed
    left = left_terms(jnp.concatenate([whole * scale, product(mixed, whole, NN)], axis=0))
    stores = []

    def store(src, dst, place):
        stores.append(pltpu.make_async_copy(src, dst, store_sem.at[place]))
        stores[-1].start()

    for i in range(steps):
        span, at = slice(i * chunk, (i + 1) * chunk), pl.ds(i * chunk, chunk)
        one, two, three = (pieces[t * size : (t + 1) * size, span] for t in range(3))
        out = dot(left, jnp.concatenate([one, three, two, one, two, one], axis=0), NN)
        basis_held[:, span] = out[:size]
        store(basis_held.at[:, at], basis.at[:, at], 2 * i)
        updated_held[:, span] = trailing[:, span] - out[size:]
        store(updated_held.at[:, at], updated.at[:, at], 2 * i + 1)
        if i == 0:
            row = lax.broadcasted_iota(jnp.int32, (size, size), 0)
            lane = lax.broadcasted_iota(jnp.int32, (size, size), 1)
            total = product(whole, gram[...], NN) + product(whole, lost, NN)
            upper_held[...] = jnp.where(row <= lane, total * (1.0 / scale), 0.0)
            store(coupling_held, coupling, 2 * steps)
            store(upper_held, upper, 2 * steps + 1)
    for copy in stores:
        copy.wait()


def shards(sizes, panel, trailing):
    size, width = panel.shape
    trail = trailing.shape[0]
    nx, ny, nz = sizes
    group = nx * ny
    rows, less = size // group, trail // group
    f32 = jnp.float32
    scale = float(width * group * nz) ** 0.5

    def params(identity=None, mebibytes=40):
        return pltpu.CompilerParams(
            collective_id=identity, has_side_effects=identity is not None, vmem_limit_bytes=mebibytes * 2**20
        )

    square = jax.ShapeDtypeStruct((size, size), f32)
    held = pl.pallas_call(
        functools.partial(reduce_kernel, sizes),
        out_shape=[
            square,
            jax.ShapeDtypeStruct((group, rows + less, size), f32),
            square,
            square,
            square,
            jax.ShapeDtypeStruct((3 * size, width), jnp.bfloat16),
            jax.ShapeDtypeStruct((trail, width), f32),
        ],
        in_specs=[HBM, HBM],
        out_specs=[VMEM] * 7,
        scratch_shapes=[
            pltpu.VMEM((size, width), f32),
            pltpu.VMEM((3 * size, width), jnp.bfloat16),
            pltpu.SemaphoreType.DMA((width // chunk_of(width, 1024) + 1,)),
            *exchange_scratch(sizes, rows, size),
            *exchange_scratch(sizes, rows + less, size),
        ],
        compiler_params=params(0),
        name="reduce",
    )(pltpu.with_memory_space_constraint(panel, pltpu.HBM), pltpu.with_memory_space_constraint(trailing, pltpu.HBM))
    basis, upper, coupling_t, updated = pl.pallas_call(
        functools.partial(final_kernel, scale),
        out_shape=[
            jax.ShapeDtypeStruct((size, width), f32),
            square,
            jax.ShapeDtypeStruct((trail, size), f32),
            jax.ShapeDtypeStruct((trail, width), f32),
        ],
        in_specs=[VMEM] * 7,
        out_specs=[HBM] * 4,
        scratch_shapes=[
            pltpu.VMEM((size, width), f32),
            pltpu.VMEM((trail, width), f32),
            pltpu.VMEM((size, size), f32),
            pltpu.VMEM((trail, size), f32),
            pltpu.SemaphoreType.DMA((2 * (width // chunk_of(width, 512)) + 2,)),
        ],
        compiler_params=params(),
        name="final",
    )(*held)
    return basis, upper, coupling_t.T, updated


def solution(mesh):
    sizes = tuple(mesh.shape[name] for name in ("gx", "gy", "gz"))
    placed = P(None, ("gx", "gy", "gz"))
    return jax.shard_map(
        functools.partial(shards, sizes),
        mesh=mesh,
        in_specs=(placed, placed),
        out_specs=(placed, P(), P(), placed),
        check_vma=False,
    )
```

```python
import functools

import jax
import jax.numpy as jnp
from jax import lax
from jax.experimental import pallas as pl
from jax.experimental.pallas import tpu as pltpu
from jax.sharding import PartitionSpec as P

MESH = pl.DeviceIdType.MESH
NT = (((1,), (1,)), ((), ()))
NN = (((1,), (0,)), ((), ()))
TN = (((0,), (0,)), ((), ()))
VMEM = pl.BlockSpec(memory_space=pltpu.VMEM)
HBM = pl.BlockSpec(memory_space=pltpu.HBM)


def dot(left, right, dims):
    return lax.dot_general(left, right, dims, preferred_element_type=jnp.float32)


def terms(value, count):
    found = []
    for _ in range(count):
        term = value.astype(jnp.bfloat16)
        found.append(term)
        value = value - term.astype(jnp.float32)
    return found


def left_terms(value):
    one, two, three = terms(value, 3)
    return jnp.concatenate([three, one, two, two, one, one], axis=1)


def right_terms(value, axis):
    one, two, three = terms(value, 3)
    return jnp.concatenate([one, three, two, one, two, one], axis=axis)


def product(left, right, dims):
    return dot(left_terms(left), right_terms(right, 1 if dims is NT else 0), dims)


def slices(value):
    top = jnp.max(jnp.abs(value), axis=1, keepdims=True) * 2.0**17
    high = (value + top) - top
    rest = value - high
    top = top * 2.0**-9
    middle = (rest + top) - top
    return high.astype(jnp.bfloat16), middle.astype(jnp.bfloat16), (rest - middle).astype(jnp.bfloat16)


def two_sum(one, two):
    total = one + two
    added = total - one
    return total, (one - (total - added)) + (two - added)


def factor(tiles, depth=8):
    size = tiles[0].shape[1]
    shape = (8, size)
    lanes = lax.broadcasted_iota(jnp.int32, shape, 1)
    row_in_tile = lax.broadcasted_iota(jnp.int32, shape, 0)
    tiles = list(tiles)
    count = len(tiles)

    def across(tile, column):
        return jnp.broadcast_to(jnp.sum(jnp.where(lanes == column, tile, 0.0), axis=1, keepdims=True), shape)

    def down(tile, row):
        return jnp.broadcast_to(tile[row : row + 1, :], shape)

    for start in range(0, count, depth):
        stop = min(start + depth, count)
        own = [across(tiles[start], 8 * start + j) for j in range(8)]
        scales = []
        for at in range(start, stop):
            first = 8 * at
            inside = (lanes >= first) & (lanes < first + 8)
            raw = list(tiles)
            columns = after = None
            if at + 1 < stop:
                columns = [across(raw[at + 1], first + j) for j in range(8)]
                after = [across(raw[at + 1], first + 8 + j) for j in range(8)]
            tile = tiles[at]
            scaled, ratios, scale = [], [], None
            for h in range(at + 1, stop):
                tiles[h] = jnp.where(inside, 0.0, tiles[h])
            for r in range(8):
                k = first + r
                pivots = {j: down(own[j], r) for j in range(r, 8)}
                over = 1.0 / pivots[r]
                scale = over if scale is None else jnp.where(row_in_tile == r, over, scale)
                ratios.append({j: pivots[j] * over for j in range(r + 1, 8)})
                unit = jnp.where(lanes == k, 1.0, down(tile, r))
                scaled.append(jnp.where(inside & (lanes > k), 0.0, unit) * over)
                if r < 7:
                    for j in range(r + 1, 8):
                        own[j] = own[j] - own[r] * ratios[r][j]
                    below = jnp.where(lanes == k, 0.0, tile) - (own[r] * over) * unit
                    tile = jnp.where(row_in_tile > r, below, tile)
                if after is not None:
                    column = columns[r]
                    for j in range(r + 1, 8):
                        columns[j] = columns[j] - column * ratios[r][j]
                    tiles[at + 1] = tiles[at + 1] - column * scaled[r]
                    times = column * over
                    for j in range(8):
                        after[j] = after[j] - times * down(column, j)
            tiles[at] = tile
            scales.append(scale)
            for h in range(at + 2, stop):
                columns = [across(raw[h], first + j) for j in range(8)]
                total = tiles[h]
                for r in range(8):
                    column = columns[r]
                    for j in range(r + 1, 8):
                        columns[j] = columns[j] - column * ratios[r][j]
                    total = total - column * scaled[r]
                tiles[h] = total
            own = after
        if stop < count:
            inner = (lanes >= 8 * start) & (lanes < 8 * stop)
            left = jnp.concatenate(tiles[start:stop], axis=0)
            right = []
            for h in range(start, stop):
                rows = row_in_tile + 8 * h
                right.append(jnp.where(lanes == rows, 1.0, jnp.where(inner & (lanes > rows), 0.0, tiles[h])) * scales[h - start])
            b1, b2, b3 = terms(jnp.concatenate(right, axis=0), 3)
            a1, a2, a3 = terms(left, 3)
            a = jnp.concatenate([a3, a1, a2, a2, a1, a1], axis=0)
            update = dot(a, jnp.concatenate([b1, b3, b2, b1, b2, b1], axis=0), TN)
            for h in range(stop, count):
                tiles[h] = jnp.where(inner, 0.0, tiles[h]) - update[8 * h : 8 * h + 8]
    uppers, inverses = [], []
    for h, tile in enumerate(tiles):
        rows = row_in_tile + 8 * h
        pivot = jnp.sum(jnp.where(lanes == rows, tile, 0.0), axis=1, keepdims=True)
        root = jnp.sqrt(pivot)
        over = 1.0 / root
        uppers.append(jnp.where(lanes > rows, tile * over, jnp.where(lanes == rows, root, 0.0)))
        inverses.append(jnp.where(lanes < rows, tile * over, jnp.where(lanes == rows, over, 0.0)))
    return uppers, inverses


def plane_peers(sizes, gx, gy):
    nx, ny, _ = sizes
    cores = 2 if ny % 2 == 0 else 1
    chips = ny // cores
    for dx in range(nx - 1, -1, -1):
        for dy in range(chips - 1, -1, -1):
            for core in range(cores):
                if (dx, dy, core) != (0, 0, 0):
                    chip = lax.rem(gy // cores + dy, chips)
                    yield lax.rem(gx + dx, nx), chip * cores + lax.rem(lax.rem(gy, cores) + core, cores)


def greet(sizes):
    nx, ny, nz = sizes
    gx, gy, gz = lax.axis_index("gx"), lax.axis_index("gy"), lax.axis_index("gz")
    barrier = pltpu.get_barrier_semaphore()
    for px, py in plane_peers(sizes, gx, gy):
        pl.semaphore_signal(barrier, inc=1, device_id=(px, py, gz), device_id_type=MESH)
    for step in range(1, nz):
        pl.semaphore_signal(barrier, inc=1, device_id=(gx, gy, lax.rem(gz + step, nz)), device_id_type=MESH)


class Exchange:
    def __init__(self, sizes, send, landed, column, gathered, send_sem, recv_sem):
        nx, ny, nz = sizes
        self.nz, self.group = nz, nx * ny
        self.send, self.landed, self.column, self.gathered = send, landed, column, gathered
        self.send_sem, self.recv_sem = send_sem, recv_sem
        gx, gy, gz = lax.axis_index("gx"), lax.axis_index("gy"), lax.axis_index("gz")
        self.me, self.gz = gx * ny + gy, gz
        me = self.me

        def copy(src, dst, at, device):
            return pltpu.make_async_remote_copy(
                src_ref=src, dst_ref=dst, send_sem=send_sem.at[at], recv_sem=recv_sem.at[at], device_id=device, device_id_type=MESH
            )

        self.out, self.back = [], []
        for slot, (px, py) in enumerate(plane_peers(sizes, gx, gy)):
            self.out.append(copy(send.at[px * ny + py], landed.at[slot], 0, (px, py, gz)))
            self.back.append(copy(gathered.at[me], gathered.at[me], 2, (px, py, gz)))
        self.along = [copy(column.at[gz], column.at[gz], 1, (gx, gy, lax.rem(gz + step, nz))) for step in range(nz - 1, 0, -1)]

    def wait(self, ref, sem):
        pltpu.make_async_copy(ref, ref, sem).wait()

    def parts(self):
        self.wait(self.landed, self.recv_sem.at[0])
        yield self.send[self.me]
        for slot in range(self.group - 1):
            yield self.landed[slot]

    def columns(self):
        self.wait(self.column.at[pl.ds(0, self.nz - 1)], self.recv_sem.at[1])
        for z in range(self.nz):
            yield self.column[z]

    def finish(self):
        self.wait(self.gathered.at[pl.ds(0, self.group - 1)], self.recv_sem.at[2])

    def drain(self):
        self.wait(self.landed, self.send_sem.at[0])
        self.wait(self.column.at[pl.ds(0, self.nz - 1)], self.send_sem.at[1])
        self.wait(self.gathered.at[pl.ds(0, self.group - 1)], self.send_sem.at[2])


def start(copies):
    for copy in copies:
        copy.start()


def sum_pairs(values):
    total, lost = None, None
    for value in values:
        if total is None:
            total = value
        else:
            total, off = two_sum(total, value)
            lost = off if lost is None else lost + off
    return total, jnp.zeros_like(total) if lost is None else lost


def sum_plain(values):
    total = None
    for value in values:
        total = value if total is None else total + value
    return total


def exchange_scratch(sizes, rows, size):
    nx, ny, nz = sizes
    group = nx * ny
    return [
        pltpu.VMEM((group, rows, size), jnp.float32),
        pltpu.VMEM((group - 1, rows, size), jnp.float32),
        pltpu.VMEM((nz, rows, size), jnp.float32),
        pltpu.VMEM((group, rows, size), jnp.float32),
        pltpu.SemaphoreType.DMA((3,)),
        pltpu.SemaphoreType.DMA((3,)),
    ]


def halves(span):
    middle = (span.start + span.stop) // 2
    return slice(span.start, middle), slice(middle, span.stop)


def chunk_of(width, most):
    return most if width % most == 0 else width


def reduce_kernel(sizes, panel, trailing, gram_out, rest_out, off_out, product_out, inverse_out, pieces, trailing_held, panel_held, sliced, move_sem, *scratch):
    size, width = panel.shape
    trail = trailing.shape[0]
    group = sizes[0] * sizes[1]
    rows, less = size // group, trail // group
    chunk = chunk_of(width, 1024)
    steps = width // chunk
    spans = [slice(i * chunk, (i + 1) * chunk) for i in range(steps)]
    loads = []
    for i in range(steps):
        at = pl.ds(i * chunk, chunk)
        loads.append(pltpu.make_async_copy(panel.at[:, at], panel_held.at[:, at], move_sem.at[i]))
    loads.append(pltpu.make_async_copy(trailing, trailing_held, move_sem.at[steps]))
    start(loads)
    greet(sizes)
    zero = jnp.zeros((size, size), jnp.float32)
    gram, lost, mixed, small = zero, zero, zero, zero
    for i in range(steps + 1):
        if i < steps:
            loads[i].wait()
            for t in range(0, size, 16):
                for place, part in enumerate(slices(panel_held[t : t + 16, spans[i]])):
                    sliced[place * size + t : place * size + t + 16, spans[i]] = part
        if i > 0:
            for half in halves(spans[i - 1]):
                found = dot(sliced[:, half], sliced[: 2 * size, half], NT)
                gram, off = two_sum(gram, found[:size, :size])
                lost = lost + off
                mixed = mixed + (found[:size, size:] + (found[2 * size :, :size] + found[2 * size :, size:]))
                small = small + found[size : 2 * size, size:]
    gram, off = two_sum(gram, small + (mixed + mixed.T))
    lost = lost + off
    heads = Exchange(sizes, *scratch[:6])
    tails = Exchange(sizes, *scratch[6:])
    for p in range(group):
        heads.send[p] = gram[p * rows : (p + 1) * rows]
    pl.semaphore_wait(pltpu.get_barrier_semaphore(), group - 1 + sizes[2] - 1)
    start(heads.out)
    loads[steps].wait()
    cross = jnp.zeros((trail, size), jnp.float32)
    for span in spans:
        both = jnp.concatenate(terms(trailing_held[:, span], 2), axis=0)
        low = sliced[2 * size :, span]
        found = dot(both, sliced[: 2 * size, span], NT)
        last = dot(jnp.concatenate([low, both], axis=0), low, NT)
        found = found[:, :size] + (found[:, size:] + last[size:])
        cross = cross + (found[:trail] + found[trail:])
        lost = lost + last[:size]
    for p in range(group):
        tails.send[p, :rows] = lost[p * rows : (p + 1) * rows]
        tails.send[p, rows:] = cross[p * less : (p + 1) * less]
    start(tails.out)
    for span in spans:
        for t in range(0, size, 16):
            for place, term in enumerate(terms(panel_held[t : t + 16, span], 3)):
                pieces[place * size + t : place * size + t + 16, span] = term
    total, lost_out = sum_pairs(heads.parts())
    heads.column[heads.gz] = total
    start(heads.along)
    part = sum_plain(tails.parts())
    tails.column[tails.gz, :rows] = part[:rows] + lost_out
    tails.column[tails.gz, rows:] = part[rows:]
    start(tails.along)
    total, lost_along = sum_pairs(heads.columns())
    heads.gathered[heads.me] = total
    start(heads.back)
    part = sum_plain(tails.columns())
    tails.gathered[tails.me, :rows] = part[:rows] + lost_along
    tails.gathered[tails.me, rows:] = part[rows:]
    start(tails.back)
    heads.finish()
    gram = jnp.concatenate([heads.gathered[p] for p in range(group)], axis=0)
    uppers, inverses = factor([gram[h : h + 8] for h in range(0, size, 8)])
    inverse = jnp.concatenate(inverses, axis=0)
    gram_out[...] = gram
    inverse_out[...] = inverse
    off, turned = departure(gram, jnp.concatenate(uppers, axis=0), inverse)
    off_out[...] = off
    product_out[...] = turned
    tails.finish()
    for p in range(group):
        rest_out[p] = tails.gathered[p]
    heads.drain()
    tails.drain()


def departure(gram, upper, inverse):
    size = gram.shape[0]
    high, middle, low = slices(upper.T)
    pair = jnp.concatenate([high, middle], axis=0)
    first = dot(pair, pair, NT)
    second = dot(low, pair, NT)
    mixed = first[:size, size:] + (second[:, :size] + second[:, size:])
    small = (first[size:, size:] + dot(low, low, NT)) + (mixed + mixed.T)
    off, lower_off = two_sum(gram, -first[:size, :size])
    lower = (high.astype(jnp.float32) + middle.astype(jnp.float32)) + low.astype(jnp.float32)
    return (off - small) + lower_off, product(inverse, lower, NN)


def refine(off, turned, inverse):
    size = off.shape[0]
    row = lax.broadcasted_iota(jnp.int32, (size, size), 0)
    lane = lax.broadcasted_iota(jnp.int32, (size, size), 1)
    moved = product(inverse, off, NN)
    second_gram = product(jnp.concatenate([turned, moved], axis=1), jnp.concatenate([turned, inverse], axis=1), NT)
    step = jnp.where(row > lane, second_gram, jnp.where(row == lane, 0.5 * second_gram - 0.5, 0.0))
    narrow = step.astype(jnp.bfloat16)
    square = dot(narrow, narrow, NN)
    twice = dot(narrow, narrow, NT)
    return (square + jnp.where(row > lane, twice, jnp.where(row == lane, 0.5 * twice, 0.0))) - step


def final_kernel(scale, gram, rest, off, turned, inverse, pieces, trailing, basis, upper, coupling, updated, basis_held, updated_held, upper_held, coupling_held, store_sem):
    size, width = basis.shape
    chunk = chunk_of(width, 512)
    steps = width // chunk
    group = rest.shape[0]
    rows = size // group
    lost = jnp.concatenate([rest[p, :rows] for p in range(group)], axis=0)
    cross = jnp.concatenate([rest[p, rows:] for p in range(group)], axis=0)
    inverse = inverse[...]
    mixed = product(cross, inverse, NT)
    change = refine(off[...] + lost, turned[...], inverse)
    whole = inverse + product(change, inverse, NN)
    mixed = mixed + product(mixed, change, NT)
    coupling_held[...] = mixed
    left = left_terms(whole * scale)
    stores = []

    def store(src, dst, place):
        stores.append(pltpu.make_async_copy(src, dst, store_sem.at[place]))
        stores[-1].start()

    for i in range(steps):
        span, at = slice(i * chunk, (i + 1) * chunk), pl.ds(i * chunk, chunk)
        one, two, three = (pieces[t * size : (t + 1) * size, span] for t in range(3))
        right = jnp.concatenate([one, three, two, one, two, one], axis=0)
        out = dot(left, right, NN)
        basis_held[:, span] = out[:size]
        store(basis_held.at[:, at], basis.at[:, at], 2 * i)
        if i == 0:
            more = left_terms(product(mixed, whole, NN))
            left = jnp.concatenate([left, more], axis=0)
            projected = dot(more, right, NN)
        else:
            projected = out[size:]
        updated_held[:, span] = trailing[:, span] - projected
        store(updated_held.at[:, at], updated.at[:, at], 2 * i + 1)
        if i == 0:
            row = lax.broadcasted_iota(jnp.int32, (size, size), 0)
            lane = lax.broadcasted_iota(jnp.int32, (size, size), 1)
            total = product(whole, gram[...], NN) + product(whole, lost, NN)
            upper_held[...] = jnp.where(row <= lane, total * (1.0 / scale), 0.0)
            store(coupling_held, coupling, 2 * steps)
            store(upper_held, upper, 2 * steps + 1)
    for copy in stores:
        copy.wait()


def shards(sizes, panel, trailing):
    size, width = panel.shape
    trail = trailing.shape[0]
    nx, ny, nz = sizes
    group = nx * ny
    rows, less = size // group, trail // group
    f32 = jnp.float32
    scale = float(width * group * nz) ** 0.5

    def params(identity=None, mebibytes=40):
        return pltpu.CompilerParams(
            collective_id=identity, has_side_effects=identity is not None, vmem_limit_bytes=mebibytes * 2**20
        )

    square = jax.ShapeDtypeStruct((size, size), f32)
    held = pl.pallas_call(
        functools.partial(reduce_kernel, sizes),
        out_shape=[
            square,
            jax.ShapeDtypeStruct((group, rows + less, size), f32),
            square,
            square,
            square,
            jax.ShapeDtypeStruct((3 * size, width), jnp.bfloat16),
            jax.ShapeDtypeStruct((trail, width), f32),
        ],
        in_specs=[HBM, HBM],
        out_specs=[VMEM] * 7,
        scratch_shapes=[
            pltpu.VMEM((size, width), f32),
            pltpu.VMEM((3 * size, width), jnp.bfloat16),
            pltpu.SemaphoreType.DMA((width // chunk_of(width, 1024) + 1,)),
            *exchange_scratch(sizes, rows, size),
            *exchange_scratch(sizes, rows + less, size),
        ],
        compiler_params=params(0),
        name="reduce",
    )(pltpu.with_memory_space_constraint(panel, pltpu.HBM), pltpu.with_memory_space_constraint(trailing, pltpu.HBM))
    basis, upper, coupling_t, updated = pl.pallas_call(
        functools.partial(final_kernel, scale),
        out_shape=[
            jax.ShapeDtypeStruct((size, width), f32),
            square,
            jax.ShapeDtypeStruct((trail, size), f32),
            jax.ShapeDtypeStruct((trail, width), f32),
        ],
        in_specs=[VMEM] * 7,
        out_specs=[HBM] * 4,
        scratch_shapes=[
            pltpu.VMEM((size, width), f32),
            pltpu.VMEM((trail, width), f32),
            pltpu.VMEM((size, size), f32),
            pltpu.VMEM((trail, size), f32),
            pltpu.SemaphoreType.DMA((2 * (width // chunk_of(width, 512)) + 2,)),
        ],
        compiler_params=params(),
        name="final",
    )(*held)
    return basis, upper, coupling_t.T, updated


def solution(mesh):
    sizes = tuple(mesh.shape[name] for name in ("gx", "gy", "gz"))
    placed = P(None, ("gx", "gy", "gz"))
    return jax.shard_map(
        functools.partial(shards, sizes),
        mesh=mesh,
        in_specs=(placed, placed),
        out_specs=(placed, P(), P(), placed),
        check_vma=False,
    )
```

```python
import functools

import jax
import jax.numpy as jnp
from jax import lax
from jax.experimental import pallas as pl
from jax.experimental.pallas import tpu as pltpu
from jax.sharding import PartitionSpec as P

MESH = pl.DeviceIdType.MESH
NT = (((1,), (1,)), ((), ()))
NN = (((1,), (0,)), ((), ()))
TN = (((0,), (0,)), ((), ()))
VMEM = pl.BlockSpec(memory_space=pltpu.VMEM)
HBM = pl.BlockSpec(memory_space=pltpu.HBM)


def dot(left, right, dims):
    return lax.dot_general(left, right, dims, preferred_element_type=jnp.float32)


def terms(value, count):
    found = []
    for _ in range(count):
        term = value.astype(jnp.bfloat16)
        found.append(term)
        value = value - term.astype(jnp.float32)
    return found


def left_terms(value):
    one, two, three = terms(value, 3)
    return jnp.concatenate([three, one, two, two, one, one], axis=1)


def right_terms(value, axis):
    one, two, three = terms(value, 3)
    return jnp.concatenate([one, three, two, one, two, one], axis=axis)


def product(left, right, dims):
    return dot(left_terms(left), right_terms(right, 1 if dims is NT else 0), dims)


def slices(value):
    top = jnp.max(jnp.abs(value), axis=1, keepdims=True) * 2.0**17
    high = (value + top) - top
    rest = value - high
    top = top * 2.0**-9
    return high, (rest + top) - top


def narrow(*values):
    return jnp.concatenate([value.astype(jnp.bfloat16) for value in values], axis=0)


def two_sum(one, two):
    total = one + two
    added = total - one
    return total, (one - (total - added)) + (two - added)


def factor(tiles, depth=8):
    size = tiles[0].shape[1]
    shape = (8, size)
    lanes = lax.broadcasted_iota(jnp.int32, shape, 1)
    row_in_tile = lax.broadcasted_iota(jnp.int32, shape, 0)
    tiles = list(tiles)
    count = len(tiles)

    def across(tile, column):
        return jnp.broadcast_to(jnp.sum(jnp.where(lanes == column, tile, 0.0), axis=1, keepdims=True), shape)

    def down(tile, row):
        return jnp.broadcast_to(tile[row : row + 1, :], shape)

    for start in range(0, count, depth):
        stop = min(start + depth, count)
        own = [across(tiles[start], 8 * start + j) for j in range(8)]
        scales = []
        for at in range(start, stop):
            first = 8 * at
            inside = (lanes >= first) & (lanes < first + 8)
            raw = list(tiles)
            columns = after = None
            if at + 1 < stop:
                columns = [across(raw[at + 1], first + j) for j in range(8)]
                after = [across(raw[at + 1], first + 8 + j) for j in range(8)]
            tile = tiles[at]
            scaled, ratios, scale = [], [], None
            for h in range(at + 1, stop):
                tiles[h] = jnp.where(inside, 0.0, tiles[h])
            for r in range(8):
                k = first + r
                pivots = {j: down(own[j], r) for j in range(r, 8)}
                over = 1.0 / pivots[r]
                scale = over if scale is None else jnp.where(row_in_tile == r, over, scale)
                ratios.append({j: pivots[j] * over for j in range(r + 1, 8)})
                unit = jnp.where(lanes == k, 1.0, down(tile, r))
                scaled.append(jnp.where(inside & (lanes > k), 0.0, unit) * over)
                if r < 7:
                    for j in range(r + 1, 8):
                        own[j] = own[j] - own[r] * ratios[r][j]
                    below = jnp.where(lanes == k, 0.0, tile) - (own[r] * over) * unit
                    tile = jnp.where(row_in_tile > r, below, tile)
                if after is not None:
                    column = columns[r]
                    for j in range(r + 1, 8):
                        columns[j] = columns[j] - column * ratios[r][j]
                    tiles[at + 1] = tiles[at + 1] - column * scaled[r]
                    times = column * over
                    for j in range(8):
                        after[j] = after[j] - times * down(column, j)
            tiles[at] = tile
            scales.append(scale)
            for h in range(at + 2, stop):
                columns = [across(raw[h], first + j) for j in range(8)]
                total = tiles[h]
                for r in range(8):
                    column = columns[r]
                    for j in range(r + 1, 8):
                        columns[j] = columns[j] - column * ratios[r][j]
                    total = total - column * scaled[r]
                tiles[h] = total
            own = after
        if stop < count:
            inner = (lanes >= 8 * start) & (lanes < 8 * stop)
            left = jnp.concatenate(tiles[start:stop], axis=0)
            right = []
            for h in range(start, stop):
                rows = row_in_tile + 8 * h
                right.append(jnp.where(lanes == rows, 1.0, jnp.where(inner & (lanes > rows), 0.0, tiles[h])) * scales[h - start])
            b1, b2, b3 = terms(jnp.concatenate(right, axis=0), 3)
            a1, a2, a3 = terms(left, 3)
            a = jnp.concatenate([a3, a1, a2, a2, a1, a1], axis=0)
            update = dot(a, jnp.concatenate([b1, b3, b2, b1, b2, b1], axis=0), TN)
            for h in range(stop, count):
                tiles[h] = jnp.where(inner, 0.0, tiles[h]) - update[8 * h : 8 * h + 8]
    uppers, inverses = [], []
    for h, tile in enumerate(tiles):
        rows = row_in_tile + 8 * h
        pivot = jnp.sum(jnp.where(lanes == rows, tile, 0.0), axis=1, keepdims=True)
        root = jnp.sqrt(pivot)
        over = 1.0 / root
        uppers.append(jnp.where(lanes > rows, tile * over, jnp.where(lanes == rows, root, 0.0)))
        inverses.append(jnp.where(lanes < rows, tile * over, jnp.where(lanes == rows, over, 0.0)))
    return uppers, inverses


def plane_peers(sizes, gx, gy):
    nx, ny, _ = sizes
    cores = 2 if ny % 2 == 0 else 1
    chips = ny // cores
    for dx in range(nx - 1, -1, -1):
        for dy in range(chips - 1, -1, -1):
            for core in range(cores):
                if (dx, dy, core) != (0, 0, 0):
                    chip = lax.rem(gy // cores + dy, chips)
                    yield lax.rem(gx + dx, nx), chip * cores + lax.rem(lax.rem(gy, cores) + core, cores)


def greet(sizes):
    nx, ny, nz = sizes
    gx, gy, gz = lax.axis_index("gx"), lax.axis_index("gy"), lax.axis_index("gz")
    barrier = pltpu.get_barrier_semaphore()
    for px, py in plane_peers(sizes, gx, gy):
        pl.semaphore_signal(barrier, inc=1, device_id=(px, py, gz), device_id_type=MESH)
    for step in range(1, nz):
        pl.semaphore_signal(barrier, inc=1, device_id=(gx, gy, lax.rem(gz + step, nz)), device_id_type=MESH)


class Exchange:
    def __init__(self, sizes, send, landed, column, gathered, send_sem, recv_sem):
        nx, ny, nz = sizes
        self.nz, self.group = nz, nx * ny
        self.send, self.landed, self.column, self.gathered = send, landed, column, gathered
        self.send_sem, self.recv_sem = send_sem, recv_sem
        gx, gy, gz = lax.axis_index("gx"), lax.axis_index("gy"), lax.axis_index("gz")
        self.me, self.gz = gx * ny + gy, gz
        me = self.me

        def copy(src, dst, at, device):
            return pltpu.make_async_remote_copy(
                src_ref=src, dst_ref=dst, send_sem=send_sem.at[at], recv_sem=recv_sem.at[at], device_id=device, device_id_type=MESH
            )

        self.out, self.back = [], []
        for slot, (px, py) in enumerate(plane_peers(sizes, gx, gy)):
            self.out.append(copy(send.at[px * ny + py], landed.at[slot], 0, (px, py, gz)))
            self.back.append(copy(gathered.at[me], gathered.at[me], 2, (px, py, gz)))
        self.along = [copy(column.at[gz], column.at[gz], 1, (gx, gy, lax.rem(gz + step, nz))) for step in range(nz - 1, 0, -1)]

    def wait(self, ref, sem):
        pltpu.make_async_copy(ref, ref, sem).wait()

    def parts(self):
        self.wait(self.landed, self.recv_sem.at[0])
        yield self.send[self.me]
        for slot in range(self.group - 1):
            yield self.landed[slot]

    def columns(self):
        self.wait(self.column.at[pl.ds(0, self.nz - 1)], self.recv_sem.at[1])
        for z in range(self.nz):
            yield self.column[z]

    def finish(self):
        self.wait(self.gathered.at[pl.ds(0, self.group - 1)], self.recv_sem.at[2])

    def drain(self):
        self.wait(self.landed, self.send_sem.at[0])
        self.wait(self.column.at[pl.ds(0, self.nz - 1)], self.send_sem.at[1])
        self.wait(self.gathered.at[pl.ds(0, self.group - 1)], self.send_sem.at[2])


def start(copies):
    for copy in copies:
        copy.start()


def sum_pairs(values):
    total, lost = None, None
    for value in values:
        if total is None:
            total = value
        else:
            total, off = two_sum(total, value)
            lost = off if lost is None else lost + off
    return total, jnp.zeros_like(total) if lost is None else lost


def sum_plain(values):
    total = None
    for value in values:
        total = value if total is None else total + value
    return total


def exchange_scratch(sizes, rows, size):
    nx, ny, nz = sizes
    group = nx * ny
    return [
        pltpu.VMEM((group, rows, size), jnp.float32),
        pltpu.VMEM((group - 1, rows, size), jnp.float32),
        pltpu.VMEM((nz, rows, size), jnp.float32),
        pltpu.VMEM((group, rows, size), jnp.float32),
        pltpu.SemaphoreType.DMA((3,)),
        pltpu.SemaphoreType.DMA((3,)),
    ]


def halves(span):
    middle = (span.start + span.stop) // 2
    return slice(span.start, middle), slice(middle, span.stop)


def chunk_of(width, most):
    return most if width % most == 0 else width


def reduce_kernel(sizes, panel, trailing, gram_out, rest_out, off_out, product_out, inverse_out, pieces, trailing_held, panel_held, move_sem, *scratch):
    size, width = panel.shape
    trail = trailing.shape[0]
    group = sizes[0] * sizes[1]
    rows, less = size // group, trail // group
    chunk = chunk_of(width, 1024)
    steps = width // chunk
    sliced = scratch[12:]
    spans = [slice(i * chunk, (i + 1) * chunk) for i in range(steps)]
    loads = []
    for i in range(steps):
        at = pl.ds(i * chunk, chunk)
        loads.append(pltpu.make_async_copy(panel.at[:, at], panel_held.at[:, at], move_sem.at[i]))
    loads.append(pltpu.make_async_copy(trailing, trailing_held, move_sem.at[steps]))
    start(loads)
    greet(sizes)
    none = lax.axis_index("gx") // sizes[0]
    zero = jnp.zeros((size, size), jnp.float32)
    gram, lost, small = zero, zero, zero
    for i in range(steps + 1):
        if i < steps:
            loads[i].wait()
            for t in range(0, size, 16):
                for place, part in enumerate(slices(panel_held[t : t + 16, spans[i]])):
                    sliced[i][0, place * size + t : place * size + t + 16] = part.astype(jnp.bfloat16)
        if i > 0:
            for half in halves(slice(0, chunk)):
                pair = sliced[i - 1][none, :, half]
                found = dot(pair, pair, NT)
                gram, off = two_sum(gram, found[:size, :size])
                lost = lost + off
                small = small + ((found[:size, size:] + found[size:, :size]) + found[size:, size:])
    gram, off = two_sum(gram, small)
    lost = lost + off
    heads = Exchange(sizes, *scratch[:6])
    tails = Exchange(sizes, *scratch[6:12])
    for p in range(group):
        heads.send[p] = gram[p * rows : (p + 1) * rows]
    pl.semaphore_wait(pltpu.get_barrier_semaphore(), group - 1 + sizes[2] - 1)
    start(heads.out)
    loads[steps].wait()
    cross = jnp.zeros((trail, size), jnp.float32)
    lows = zero
    for i, span in enumerate(spans):
        pair = sliced[i][none]
        low = (panel_held[:, span] - pair[:size].astype(jnp.float32)) - pair[size:].astype(jnp.float32)
        low = low.astype(jnp.bfloat16)
        one, two = terms(trailing_held[:, span], 2)
        left = jnp.concatenate([low, one, two], axis=0)
        found = dot(left, pair, NT)
        last = dot(left, low, NT)
        found = found[:, :size] + found[:, size:]
        lows = lows + found[:size]
        lost = lost + last[:size]
        found = found[size:] + last[size:]
        cross = cross + (found[:trail] + found[trail:])
    lost = lost + (lows + lows.T)
    for p in range(group):
        tails.send[p, :rows] = lost[p * rows : (p + 1) * rows]
        tails.send[p, rows:] = cross[p * less : (p + 1) * less]
    start(tails.out)
    for span in spans:
        for t in range(0, size, 16):
            for place, term in enumerate(terms(panel_held[t : t + 16, span], 3)):
                pieces[place * size + t : place * size + t + 16, span] = term
    total, lost_out = sum_pairs(heads.parts())
    heads.column[heads.gz] = total
    start(heads.along)
    part = sum_plain(tails.parts())
    tails.column[tails.gz, :rows] = part[:rows] + lost_out
    tails.column[tails.gz, rows:] = part[rows:]
    start(tails.along)
    total, lost_along = sum_pairs(heads.columns())
    heads.gathered[heads.me] = total
    start(heads.back)
    part = sum_plain(tails.columns())
    tails.gathered[tails.me, :rows] = part[:rows] + lost_along
    tails.gathered[tails.me, rows:] = part[rows:]
    start(tails.back)
    heads.finish()
    gram = jnp.concatenate([heads.gathered[p] for p in range(group)], axis=0)
    uppers, inverses = factor([gram[h : h + 8] for h in range(0, size, 8)])
    inverse = jnp.concatenate(inverses, axis=0)
    gram_out[...] = gram
    inverse_out[...] = inverse
    off, turned = departure(gram, jnp.concatenate(uppers, axis=0), inverse)
    off_out[...] = off
    product_out[...] = turned
    tails.finish()
    for p in range(group):
        rest_out[p] = tails.gathered[p]
    heads.drain()
    tails.drain()


def departure(gram, upper, inverse):
    size = gram.shape[0]
    lower = upper.T
    high, middle = slices(lower)
    low = ((lower - high) - middle).astype(jnp.bfloat16)
    pair = narrow(high, middle)
    first = dot(pair, pair, NT)
    second = dot(low, pair, NT)
    mixed = first[:size, size:] + (second[:, :size] + second[:, size:])
    small = (first[size:, size:] + dot(low, low, NT)) + (mixed + mixed.T)
    off, lower_off = two_sum(gram, -first[:size, :size])
    lower = (high + middle) + low.astype(jnp.float32)
    return (off - small) + lower_off, product(inverse, lower, NN)


def refine(off, turned, inverse):
    size = off.shape[0]
    row = lax.broadcasted_iota(jnp.int32, (size, size), 0)
    lane = lax.broadcasted_iota(jnp.int32, (size, size), 1)
    moved = product(inverse, off, NN)
    second_gram = product(jnp.concatenate([turned, moved], axis=1), jnp.concatenate([turned, inverse], axis=1), NT)
    step = jnp.where(row > lane, second_gram, jnp.where(row == lane, 0.5 * second_gram - 0.5, 0.0))
    rough = step.astype(jnp.bfloat16)
    square = dot(rough, rough, NN)
    twice = dot(rough, rough, NT)
    return (square + jnp.where(row > lane, twice, jnp.where(row == lane, 0.5 * twice, 0.0))) - step


def final_kernel(scale, gram, rest, off, turned, inverse, pieces, trailing, basis, upper, coupling, updated, basis_held, updated_held, upper_held, coupling_held, store_sem):
    size, width = basis.shape
    chunk = chunk_of(width, 512)
    steps = width // chunk
    group = rest.shape[0]
    rows = size // group
    lost = jnp.concatenate([rest[p, :rows] for p in range(group)], axis=0)
    cross = jnp.concatenate([rest[p, rows:] for p in range(group)], axis=0)
    inverse = inverse[...]
    mixed = product(cross, inverse, NT)
    change = refine(off[...] + lost, turned[...], inverse)
    whole = inverse + product(change, inverse, NN)
    mixed = mixed + product(mixed, change, NT)
    coupling_held[...] = mixed
    left = left_terms(whole * scale)
    stores = []

    def store(src, dst, place):
        stores.append(pltpu.make_async_copy(src, dst, store_sem.at[place]))
        stores[-1].start()

    for i in range(steps):
        span, at = slice(i * chunk, (i + 1) * chunk), pl.ds(i * chunk, chunk)
        one, two, three = (pieces[t * size : (t + 1) * size, span] for t in range(3))
        right = jnp.concatenate([one, three, two, one, two, one], axis=0)
        out = dot(left, right, NN)
        basis_held[:, span] = out[:size]
        store(basis_held.at[:, at], basis.at[:, at], 2 * i)
        if i == 0:
            more = left_terms(product(mixed, whole, NN))
            left = jnp.concatenate([left, more], axis=0)
            projected = dot(more, right, NN)
        else:
            projected = out[size:]
        updated_held[:, span] = trailing[:, span] - projected
        store(updated_held.at[:, at], updated.at[:, at], 2 * i + 1)
        if i == 0:
            row = lax.broadcasted_iota(jnp.int32, (size, size), 0)
            lane = lax.broadcasted_iota(jnp.int32, (size, size), 1)
            total = product(whole, gram[...], NN) + product(whole, lost, NN)
            upper_held[...] = jnp.where(row <= lane, total * (1.0 / scale), 0.0)
            store(coupling_held, coupling, 2 * steps)
            store(upper_held, upper, 2 * steps + 1)
    for copy in stores:
        copy.wait()


def shards(sizes, panel, trailing):
    size, width = panel.shape
    trail = trailing.shape[0]
    nx, ny, nz = sizes
    group = nx * ny
    rows, less = size // group, trail // group
    f32 = jnp.float32
    scale = float(width * group * nz) ** 0.5

    def params(identity=None, mebibytes=40):
        return pltpu.CompilerParams(
            collective_id=identity, has_side_effects=identity is not None, vmem_limit_bytes=mebibytes * 2**20
        )

    square = jax.ShapeDtypeStruct((size, size), f32)
    held = pl.pallas_call(
        functools.partial(reduce_kernel, sizes),
        out_shape=[
            square,
            jax.ShapeDtypeStruct((group, rows + less, size), f32),
            square,
            square,
            square,
            jax.ShapeDtypeStruct((3 * size, width), jnp.bfloat16),
            jax.ShapeDtypeStruct((trail, width), f32),
        ],
        in_specs=[HBM, HBM],
        out_specs=[VMEM] * 7,
        scratch_shapes=[
            pltpu.VMEM((size, width), f32),
            pltpu.SemaphoreType.DMA((width // chunk_of(width, 1024) + 1,)),
            *exchange_scratch(sizes, rows, size),
            *exchange_scratch(sizes, rows + less, size),
            *[pltpu.VMEM((1, 2 * size, chunk_of(width, 1024)), jnp.bfloat16) for _ in range(width // chunk_of(width, 1024))],
        ],
        compiler_params=params(0),
        name="reduce",
    )(pltpu.with_memory_space_constraint(panel, pltpu.HBM), pltpu.with_memory_space_constraint(trailing, pltpu.HBM))
    basis, upper, coupling_t, updated = pl.pallas_call(
        functools.partial(final_kernel, scale),
        out_shape=[
            jax.ShapeDtypeStruct((size, width), f32),
            square,
            jax.ShapeDtypeStruct((trail, size), f32),
            jax.ShapeDtypeStruct((trail, width), f32),
        ],
        in_specs=[VMEM] * 7,
        out_specs=[HBM] * 4,
        scratch_shapes=[
            pltpu.VMEM((size, width), f32),
            pltpu.VMEM((trail, width), f32),
            pltpu.VMEM((size, size), f32),
            pltpu.VMEM((trail, size), f32),
            pltpu.SemaphoreType.DMA((2 * (width // chunk_of(width, 512)) + 2,)),
        ],
        compiler_params=params(),
        name="final",
    )(*held)
    return basis, upper, coupling_t.T, updated


def solution(mesh):
    sizes = tuple(mesh.shape[name] for name in ("gx", "gy", "gz"))
    placed = P(None, ("gx", "gy", "gz"))
    return jax.shard_map(
        functools.partial(shards, sizes),
        mesh=mesh,
        in_specs=(placed, placed),
        out_specs=(placed, P(), P(), placed),
        check_vma=False,
    )
```

```python
import functools

import jax
import jax.numpy as jnp
from jax import lax
from jax.experimental import pallas as pl
from jax.experimental.pallas import tpu as pltpu
from jax.sharding import PartitionSpec as P

MESH = pl.DeviceIdType.MESH
NT = (((1,), (1,)), ((), ()))
NN = (((1,), (0,)), ((), ()))
TN = (((0,), (0,)), ((), ()))
VMEM = pl.BlockSpec(memory_space=pltpu.VMEM)
HBM = pl.BlockSpec(memory_space=pltpu.HBM)


def dot(left, right, dims):
    return lax.dot_general(left, right, dims, preferred_element_type=jnp.float32)


def terms(value, count):
    found = []
    for _ in range(count):
        term = value.astype(jnp.bfloat16)
        found.append(term)
        value = value - term.astype(jnp.float32)
    return found


def left_terms(value):
    one, two, three = terms(value, 3)
    return jnp.concatenate([three, one, two, two, one, one], axis=1)


def right_terms(value, axis):
    one, two, three = terms(value, 3)
    return jnp.concatenate([one, three, two, one, two, one], axis=axis)


def product(left, right, dims):
    return dot(left_terms(left), right_terms(right, 1 if dims is NT else 0), dims)


def slices(value):
    top = jnp.max(jnp.abs(value), axis=1, keepdims=True) * 2.0**17
    high = (value + top) - top
    rest = value - high
    top = top * 2.0**-9
    return high, (rest + top) - top


def narrow(*values):
    return jnp.concatenate([value.astype(jnp.bfloat16) for value in values], axis=0)


def two_sum(one, two):
    total = one + two
    added = total - one
    return total, (one - (total - added)) + (two - added)


def factor(tiles, depth=8):
    size = tiles[0].shape[1]
    shape = (8, size)
    lanes = lax.broadcasted_iota(jnp.int32, shape, 1)
    row_in_tile = lax.broadcasted_iota(jnp.int32, shape, 0)
    tiles = list(tiles)
    count = len(tiles)

    def across(tile, column):
        return jnp.broadcast_to(jnp.sum(jnp.where(lanes == column, tile, 0.0), axis=1, keepdims=True), shape)

    def down(tile, row):
        return jnp.broadcast_to(tile[row : row + 1, :], shape)

    for start in range(0, count, depth):
        stop = min(start + depth, count)
        own = [across(tiles[start], 8 * start + j) for j in range(8)]
        scales = []
        for at in range(start, stop):
            first = 8 * at
            inside = (lanes >= first) & (lanes < first + 8)
            raw = list(tiles)
            columns = after = None
            if at + 1 < stop:
                columns = [across(raw[at + 1], first + j) for j in range(8)]
                after = [across(raw[at + 1], first + 8 + j) for j in range(8)]
            tile = tiles[at]
            scaled, ratios, scale = [], [], None
            for h in range(at + 1, stop):
                tiles[h] = jnp.where(inside, 0.0, tiles[h])
            for r in range(8):
                k = first + r
                pivots = {j: down(own[j], r) for j in range(r, 8)}
                over = 1.0 / pivots[r]
                scale = over if scale is None else jnp.where(row_in_tile == r, over, scale)
                ratios.append({j: pivots[j] * over for j in range(r + 1, 8)})
                unit = jnp.where(lanes == k, 1.0, down(tile, r))
                scaled.append(jnp.where(inside & (lanes > k), 0.0, unit) * over)
                if r < 7:
                    for j in range(r + 1, 8):
                        own[j] = own[j] - own[r] * ratios[r][j]
                    below = jnp.where(lanes == k, 0.0, tile) - (own[r] * over) * unit
                    tile = jnp.where(row_in_tile > r, below, tile)
                if after is not None:
                    column = columns[r]
                    for j in range(r + 1, 8):
                        columns[j] = columns[j] - column * ratios[r][j]
                    tiles[at + 1] = tiles[at + 1] - column * scaled[r]
                    times = column * over
                    for j in range(8):
                        after[j] = after[j] - times * down(column, j)
            tiles[at] = tile
            scales.append(scale)
            for h in range(at + 2, stop):
                columns = [across(raw[h], first + j) for j in range(8)]
                total = tiles[h]
                for r in range(8):
                    column = columns[r]
                    for j in range(r + 1, 8):
                        columns[j] = columns[j] - column * ratios[r][j]
                    total = total - column * scaled[r]
                tiles[h] = total
            own = after
        if stop < count:
            inner = (lanes >= 8 * start) & (lanes < 8 * stop)
            left = jnp.concatenate(tiles[start:stop], axis=0)
            right = []
            for h in range(start, stop):
                rows = row_in_tile + 8 * h
                right.append(jnp.where(lanes == rows, 1.0, jnp.where(inner & (lanes > rows), 0.0, tiles[h])) * scales[h - start])
            b1, b2, b3 = terms(jnp.concatenate(right, axis=0), 3)
            a1, a2, a3 = terms(left, 3)
            a = jnp.concatenate([a3, a1, a2, a2, a1, a1], axis=0)
            update = dot(a, jnp.concatenate([b1, b3, b2, b1, b2, b1], axis=0), TN)
            for h in range(stop, count):
                tiles[h] = jnp.where(inner, 0.0, tiles[h]) - update[8 * h : 8 * h + 8]
    uppers, inverses = [], []
    for h, tile in enumerate(tiles):
        rows = row_in_tile + 8 * h
        pivot = jnp.sum(jnp.where(lanes == rows, tile, 0.0), axis=1, keepdims=True)
        root = jnp.sqrt(pivot)
        over = 1.0 / root
        uppers.append(jnp.where(lanes > rows, tile * over, jnp.where(lanes == rows, root, 0.0)))
        inverses.append(jnp.where(lanes < rows, tile * over, jnp.where(lanes == rows, over, 0.0)))
    return uppers, inverses


def plane_peers(sizes, gx, gy):
    nx, ny, _ = sizes
    cores = 2 if ny % 2 == 0 else 1
    chips = ny // cores
    for dx in range(nx - 1, -1, -1):
        for dy in range(chips - 1, -1, -1):
            for core in range(cores):
                if (dx, dy, core) != (0, 0, 0):
                    chip = lax.rem(gy // cores + dy, chips)
                    yield lax.rem(gx + dx, nx), chip * cores + lax.rem(lax.rem(gy, cores) + core, cores)


def greet(sizes):
    nx, ny, nz = sizes
    gx, gy, gz = lax.axis_index("gx"), lax.axis_index("gy"), lax.axis_index("gz")
    barrier = pltpu.get_barrier_semaphore()
    for px, py in plane_peers(sizes, gx, gy):
        pl.semaphore_signal(barrier, inc=1, device_id=(px, py, gz), device_id_type=MESH)
    for step in range(1, nz):
        pl.semaphore_signal(barrier, inc=1, device_id=(gx, gy, lax.rem(gz + step, nz)), device_id_type=MESH)


class Exchange:
    def __init__(self, sizes, send, landed, column, gathered, send_sem, recv_sem):
        nx, ny, nz = sizes
        self.nz, self.group = nz, nx * ny
        self.send, self.landed, self.column, self.gathered = send, landed, column, gathered
        self.send_sem, self.recv_sem = send_sem, recv_sem
        gx, gy, gz = lax.axis_index("gx"), lax.axis_index("gy"), lax.axis_index("gz")
        self.me, self.gz = gx * ny + gy, gz
        me = self.me

        def copy(src, dst, at, device):
            return pltpu.make_async_remote_copy(
                src_ref=src, dst_ref=dst, send_sem=send_sem.at[at], recv_sem=recv_sem.at[at], device_id=device, device_id_type=MESH
            )

        self.out, self.back = [], []
        for slot, (px, py) in enumerate(plane_peers(sizes, gx, gy)):
            self.out.append(copy(send.at[px * ny + py], landed.at[slot], 0, (px, py, gz)))
            self.back.append(copy(gathered.at[me], gathered.at[me], 2, (px, py, gz)))
        self.along = [copy(column.at[gz], column.at[gz], 1, (gx, gy, lax.rem(gz + step, nz))) for step in range(nz - 1, 0, -1)]

    def wait(self, ref, sem):
        pltpu.make_async_copy(ref, ref, sem).wait()

    def parts(self):
        self.wait(self.landed, self.recv_sem.at[0])
        yield self.send[self.me]
        for slot in range(self.group - 1):
            yield self.landed[slot]

    def columns(self):
        self.wait(self.column.at[pl.ds(0, self.nz - 1)], self.recv_sem.at[1])
        for z in range(self.nz):
            yield self.column[z]

    def finish(self):
        self.wait(self.gathered.at[pl.ds(0, self.group - 1)], self.recv_sem.at[2])

    def drain(self):
        self.wait(self.landed, self.send_sem.at[0])
        self.wait(self.column.at[pl.ds(0, self.nz - 1)], self.send_sem.at[1])
        self.wait(self.gathered.at[pl.ds(0, self.group - 1)], self.send_sem.at[2])


def start(copies):
    for copy in copies:
        copy.start()


def sum_pairs(values):
    total, lost = None, None
    for value in values:
        if total is None:
            total = value
        else:
            total, off = two_sum(total, value)
            lost = off if lost is None else lost + off
    return total, jnp.zeros_like(total) if lost is None else lost


def sum_plain(values):
    total = None
    for value in values:
        total = value if total is None else total + value
    return total


def exchange_scratch(sizes, rows, size):
    nx, ny, nz = sizes
    group = nx * ny
    return [
        pltpu.VMEM((group, rows, size), jnp.float32),
        pltpu.VMEM((group - 1, rows, size), jnp.float32),
        pltpu.VMEM((nz, rows, size), jnp.float32),
        pltpu.VMEM((group, rows, size), jnp.float32),
        pltpu.SemaphoreType.DMA((3,)),
        pltpu.SemaphoreType.DMA((3,)),
    ]


def halves(span):
    middle = (span.start + span.stop) // 2
    return slice(span.start, middle), slice(middle, span.stop)


def chunk_of(width, most):
    return most if width % most == 0 else width


def spans_of(width):
    chunk = chunk_of(width, 1024)
    return [slice(at, at + chunk) for at in range(0, width, chunk)]


def reduce_kernel(sizes, panel, trailing, gram_out, rest_out, upper_out, inverse_out, pieces, trailing_held, panel_held, move_sem, *scratch):
    size, width = panel.shape
    trail = trailing.shape[0]
    group = sizes[0] * sizes[1]
    rows, less = size // group, trail // group
    spans = spans_of(width)
    steps = len(spans)
    sliced = scratch[12:]
    loads = []
    for i, span in enumerate(spans):
        at = pl.ds(span.start, span.stop - span.start)
        loads.append(pltpu.make_async_copy(panel.at[:, at], panel_held.at[:, at], move_sem.at[i]))
    loads.append(pltpu.make_async_copy(trailing, trailing_held, move_sem.at[steps]))
    start(loads)
    greet(sizes)
    none = lax.axis_index("gx") // sizes[0]
    zero = jnp.zeros((size, size), jnp.float32)
    gram, lost, small = zero, zero, zero
    for i in range(steps + 1):
        if i < steps:
            loads[i].wait()
            for t in range(0, size, 16):
                for place, part in enumerate(slices(panel_held[t : t + 16, spans[i]])):
                    sliced[i][0, place * size + t : place * size + t + 16] = part.astype(jnp.bfloat16)
        if i > 0:
            for half in halves(slice(0, spans[i - 1].stop - spans[i - 1].start)):
                pair = sliced[i - 1][none, :, half]
                found = dot(pair, pair, NT)
                gram, off = two_sum(gram, found[:size, :size])
                lost = lost + off
                small = small + ((found[:size, size:] + found[size:, :size]) + found[size:, size:])
    gram, off = two_sum(gram, small)
    lost = lost + off
    heads = Exchange(sizes, *scratch[:6])
    tails = Exchange(sizes, *scratch[6:12])
    for p in range(group):
        heads.send[p] = gram[p * rows : (p + 1) * rows]
    pl.semaphore_wait(pltpu.get_barrier_semaphore(), group - 1 + sizes[2] - 1)
    start(heads.out)
    loads[steps].wait()
    cross = jnp.zeros((trail, size), jnp.float32)
    lows = zero
    for i, span in enumerate(spans):
        pair = sliced[i][none]
        low = (panel_held[:, span] - pair[:size].astype(jnp.float32)) - pair[size:].astype(jnp.float32)
        low = low.astype(jnp.bfloat16)
        one, two = terms(trailing_held[:, span], 2)
        left = jnp.concatenate([low, one, two], axis=0)
        found = dot(left, pair, NT)
        last = dot(left, low, NT)
        found = found[:, :size] + found[:, size:]
        lows = lows + found[:size]
        lost = lost + last[:size]
        found = found[size:] + last[size:]
        cross = cross + (found[:trail] + found[trail:])
    lost = lost + (lows + lows.T)
    for p in range(group):
        tails.send[p, :rows] = lost[p * rows : (p + 1) * rows]
        tails.send[p, rows:] = cross[p * less : (p + 1) * less]
    start(tails.out)
    for span in spans:
        for t in range(0, size, 16):
            for place, term in enumerate(terms(panel_held[t : t + 16, span], 3)):
                pieces[place * size + t : place * size + t + 16, span] = term
    total, lost_out = sum_pairs(heads.parts())
    heads.column[heads.gz] = total
    start(heads.along)
    part = sum_plain(tails.parts())
    tails.column[tails.gz, :rows] = part[:rows] + lost_out
    tails.column[tails.gz, rows:] = part[rows:]
    start(tails.along)
    total, lost_along = sum_pairs(heads.columns())
    heads.gathered[heads.me] = total
    start(heads.back)
    part = sum_plain(tails.columns())
    tails.gathered[tails.me, :rows] = part[:rows] + lost_along
    tails.gathered[tails.me, rows:] = part[rows:]
    start(tails.back)
    heads.finish()
    gram = jnp.concatenate([heads.gathered[p] for p in range(group)], axis=0)
    uppers, inverses = factor([gram[h : h + 8] for h in range(0, size, 8)])
    gram_out[...] = gram
    upper_out[...] = jnp.concatenate(uppers, axis=0)
    inverse_out[...] = jnp.concatenate(inverses, axis=0)
    tails.finish()
    for p in range(group):
        rest_out[p] = tails.gathered[p]
    heads.drain()
    tails.drain()


def departure(gram, upper, inverse):
    size = gram.shape[0]
    lower = upper.T
    high, middle = slices(lower)
    low = ((lower - high) - middle).astype(jnp.bfloat16)
    pair = narrow(high, middle)
    first = dot(pair, pair, NT)
    second = dot(low, pair, NT)
    mixed = first[:size, size:] + (second[:, :size] + second[:, size:])
    small = (first[size:, size:] + dot(low, low, NT)) + (mixed + mixed.T)
    off, lower_off = two_sum(gram, -first[:size, :size])
    lower = (high + middle) + low.astype(jnp.float32)
    return (off - small) + lower_off, product(inverse, lower, NN)


def refine(off, turned, inverse):
    size = off.shape[0]
    row = lax.broadcasted_iota(jnp.int32, (size, size), 0)
    lane = lax.broadcasted_iota(jnp.int32, (size, size), 1)
    moved = product(inverse, off, NN)
    second_gram = product(jnp.concatenate([turned, moved], axis=1), jnp.concatenate([turned, inverse], axis=1), NT)
    step = jnp.where(row > lane, second_gram, jnp.where(row == lane, 0.5 * second_gram - 0.5, 0.0))
    rough = step.astype(jnp.bfloat16)
    square = dot(rough, rough, NN)
    twice = dot(rough, rough, NT)
    return (square + jnp.where(row > lane, twice, jnp.where(row == lane, 0.5 * twice, 0.0))) - step


def final_kernel(scale, gram, rest, first_upper, inverse, pieces, trailing, basis, upper, coupling, updated, basis_held, updated_held, upper_held, coupling_held, both_held, store_sem):
    size, width = basis.shape
    chunk = chunk_of(width, 512)
    steps = width // chunk
    group = rest.shape[0]
    rows = size // group
    lost = jnp.concatenate([rest[p, :rows] for p in range(group)], axis=0)
    cross = jnp.concatenate([rest[p, rows:] for p in range(group)], axis=0)
    gram, inverse = gram[...], inverse[...]
    off, turned = departure(gram, first_upper[...], inverse)
    mixed = product(cross, inverse, NT)
    left = left_terms(inverse * scale)
    for i in range(steps):
        span = slice(i * chunk, (i + 1) * chunk)
        one, two, three = (pieces[t * size : (t + 1) * size, span] for t in range(3))
        first = dot(left, jnp.concatenate([one, three, two, one, two, one], axis=0), NN)
        basis_held[:, span] = first
        one, two = terms(first, 2)
        both_held[:size, span] = one
        both_held[size:, span] = two
    change = refine(off + lost, turned, inverse)
    mixed = mixed + product(mixed, change, NT)
    coupling_held[...] = mixed
    back = (mixed + product(mixed, change, NN)) * (1.0 / scale)
    one, two = terms(back, 2)
    rough = change.astype(jnp.bfloat16)
    left = jnp.concatenate(
        [
            jnp.concatenate([rough, rough], axis=1),
            jnp.concatenate([one, one], axis=1),
            jnp.concatenate([two, jnp.zeros_like(two)], axis=1),
        ],
        axis=0,
    )
    stores = []

    def store(src, dst, place):
        stores.append(pltpu.make_async_copy(src, dst, store_sem.at[place]))
        stores[-1].start()

    for i in range(steps):
        span, at = slice(i * chunk, (i + 1) * chunk), pl.ds(i * chunk, chunk)
        out = dot(left, both_held[:, span], NN)
        basis_held[:, span] = basis_held[:, span] + out[:size]
        store(basis_held.at[:, at], basis.at[:, at], 2 * i)
        updated_held[:, span] = trailing[:, span] - (out[size : size + back.shape[0]] + out[size + back.shape[0] :])
        store(updated_held.at[:, at], updated.at[:, at], 2 * i + 1)
        if i == 0:
            row = lax.broadcasted_iota(jnp.int32, (size, size), 0)
            lane = lax.broadcasted_iota(jnp.int32, (size, size), 1)
            whole = inverse + product(change, inverse, NN)
            total = product(whole, gram, NN) + product(whole, lost, NN)
            upper_held[...] = jnp.where(row <= lane, total * (1.0 / scale), 0.0)
            store(coupling_held, coupling, 2 * steps)
            store(upper_held, upper, 2 * steps + 1)
    for copy in stores:
        copy.wait()


def shards(sizes, panel, trailing):
    size, width = panel.shape
    trail = trailing.shape[0]
    nx, ny, nz = sizes
    group = nx * ny
    rows, less = size // group, trail // group
    f32 = jnp.float32
    scale = float(width * group * nz) ** 0.5

    def params(identity=None, mebibytes=40):
        return pltpu.CompilerParams(
            collective_id=identity, has_side_effects=identity is not None, vmem_limit_bytes=mebibytes * 2**20
        )

    square = jax.ShapeDtypeStruct((size, size), f32)
    held = pl.pallas_call(
        functools.partial(reduce_kernel, sizes),
        out_shape=[
            square,
            jax.ShapeDtypeStruct((group, rows + less, size), f32),
            square,
            square,
            jax.ShapeDtypeStruct((3 * size, width), jnp.bfloat16),
            jax.ShapeDtypeStruct((trail, width), f32),
        ],
        in_specs=[HBM, HBM],
        out_specs=[VMEM] * 6,
        scratch_shapes=[
            pltpu.VMEM((size, width), f32),
            pltpu.SemaphoreType.DMA((len(spans_of(width)) + 1,)),
            *exchange_scratch(sizes, rows, size),
            *exchange_scratch(sizes, rows + less, size),
            *[pltpu.VMEM((1, 2 * size, span.stop - span.start), jnp.bfloat16) for span in spans_of(width)],
        ],
        compiler_params=params(0),
        name="reduce",
    )(pltpu.with_memory_space_constraint(panel, pltpu.HBM), pltpu.with_memory_space_constraint(trailing, pltpu.HBM))
    basis, upper, coupling_t, updated = pl.pallas_call(
        functools.partial(final_kernel, scale),
        out_shape=[
            jax.ShapeDtypeStruct((size, width), f32),
            square,
            jax.ShapeDtypeStruct((trail, size), f32),
            jax.ShapeDtypeStruct((trail, width), f32),
        ],
        in_specs=[VMEM] * 6,
        out_specs=[HBM] * 4,
        scratch_shapes=[
            pltpu.VMEM((size, width), f32),
            pltpu.VMEM((trail, width), f32),
            pltpu.VMEM((size, size), f32),
            pltpu.VMEM((trail, size), f32),
            pltpu.VMEM((2 * size, width), jnp.bfloat16),
            pltpu.SemaphoreType.DMA((2 * (width // chunk_of(width, 512)) + 2,)),
        ],
        compiler_params=params(),
        name="final",
    )(*held)
    return basis, upper, coupling_t.T, updated


def solution(mesh):
    sizes = tuple(mesh.shape[name] for name in ("gx", "gy", "gz"))
    placed = P(None, ("gx", "gy", "gz"))
    return jax.shard_map(
        functools.partial(shards, sizes),
        mesh=mesh,
        in_specs=(placed, placed),
        out_specs=(placed, P(), P(), placed),
        check_vma=False,
    )
```

```python
import functools

import jax
import jax.numpy as jnp
from jax import lax
from jax.experimental import pallas as pl
from jax.experimental.pallas import tpu as pltpu
from jax.sharding import PartitionSpec as P

MESH = pl.DeviceIdType.MESH
NT = (((1,), (1,)), ((), ()))
NN = (((1,), (0,)), ((), ()))
TN = (((0,), (0,)), ((), ()))
VMEM = pl.BlockSpec(memory_space=pltpu.VMEM)
HBM = pl.BlockSpec(memory_space=pltpu.HBM)


def dot(left, right, dims):
    return lax.dot_general(left, right, dims, preferred_element_type=jnp.float32)


def terms(value, count):
    found = []
    for _ in range(count):
        term = value.astype(jnp.bfloat16)
        found.append(term)
        value = value - term.astype(jnp.float32)
    return found


def left_terms(value):
    one, two, three = terms(value, 3)
    return jnp.concatenate([three, one, two, two, one, one], axis=1)


def right_terms(value, axis):
    one, two, three = terms(value, 3)
    return jnp.concatenate([one, three, two, one, two, one], axis=axis)


def product(left, right, dims):
    return dot(left_terms(left), right_terms(right, 1 if dims is NT else 0), dims)


def close_product(left, right, dims):
    one, two = terms(left, 2)
    first, second = terms(right, 2)
    axis = 1 if dims is NT else 0
    return dot(jnp.concatenate([two, one, one], axis=1), jnp.concatenate([first, second, first], axis=axis), dims)


def slices(value):
    top = jnp.max(jnp.abs(value), axis=1, keepdims=True) * 2.0**17
    high = (value + top) - top
    rest = value - high
    top = top * 2.0**-9
    return high, (rest + top) - top


def narrow(*values):
    return jnp.concatenate([value.astype(jnp.bfloat16) for value in values], axis=0)


def two_sum(one, two):
    total = one + two
    added = total - one
    return total, (one - (total - added)) + (two - added)


def factor(tiles, depth=8):
    size = tiles[0].shape[1]
    shape = (8, size)
    lanes = lax.broadcasted_iota(jnp.int32, shape, 1)
    row_in_tile = lax.broadcasted_iota(jnp.int32, shape, 0)
    tiles = list(tiles)
    count = len(tiles)
    every = []

    def across(tile, column):
        return jnp.broadcast_to(jnp.sum(jnp.where(lanes == column, tile, 0.0), axis=1, keepdims=True), shape)

    def down(tile, row):
        return jnp.broadcast_to(tile[row : row + 1, :], shape)

    for start in range(0, count, depth):
        stop = min(start + depth, count)
        own = [across(tiles[start], 8 * start + j) for j in range(8)]
        scales = []
        for at in range(start, stop):
            first = 8 * at
            inside = (lanes >= first) & (lanes < first + 8)
            raw = list(tiles)
            columns = after = None
            if at + 1 < stop:
                columns = [across(raw[at + 1], first + j) for j in range(8)]
                after = [across(raw[at + 1], first + 8 + j) for j in range(8)]
            tile = tiles[at]
            scaled, ratios, scale = [], [], None
            for h in range(at + 1, stop):
                tiles[h] = jnp.where(inside, 0.0, tiles[h])
            for r in range(8):
                k = first + r
                pivots = {j: down(own[j], r) for j in range(r, 8)}
                over = 1.0 / pivots[r]
                scale = over if scale is None else jnp.where(row_in_tile == r, over, scale)
                ratios.append({j: pivots[j] * over for j in range(r + 1, 8)})
                unit = jnp.where(lanes == k, 1.0, down(tile, r))
                scaled.append(jnp.where(inside & (lanes > k), 0.0, unit) * over)
                if r < 7:
                    for j in range(r + 1, 8):
                        own[j] = own[j] - own[r] * ratios[r][j]
                    below = jnp.where(lanes == k, 0.0, tile) - (own[r] * over) * unit
                    tile = jnp.where(row_in_tile > r, below, tile)
                if after is not None:
                    column = columns[r]
                    for j in range(r + 1, 8):
                        columns[j] = columns[j] - column * ratios[r][j]
                    tiles[at + 1] = tiles[at + 1] - column * scaled[r]
                    times = column * over
                    for j in range(8):
                        after[j] = after[j] - times * down(column, j)
            tiles[at] = tile
            scales.append(scale)
            every.append(scale)
            for h in range(at + 2, stop):
                columns = [across(raw[h], first + j) for j in range(8)]
                total = tiles[h]
                for r in range(8):
                    column = columns[r]
                    for j in range(r + 1, 8):
                        columns[j] = columns[j] - column * ratios[r][j]
                    total = total - column * scaled[r]
                tiles[h] = total
            own = after
        if stop < count:
            inner = (lanes >= 8 * start) & (lanes < 8 * stop)
            left = jnp.concatenate(tiles[start:stop], axis=0)
            right = []
            for h in range(start, stop):
                rows = row_in_tile + 8 * h
                right.append(jnp.where(lanes == rows, 1.0, jnp.where(inner & (lanes > rows), 0.0, tiles[h])) * scales[h - start])
            b1, b2, b3 = terms(jnp.concatenate(right, axis=0), 3)
            a1, a2, a3 = terms(left, 3)
            update = dot(jnp.concatenate([a3, a1, a2], axis=0), jnp.concatenate([b1, b3, b2], axis=0), TN)
            update = update + dot(jnp.concatenate([a2, a1, a1], axis=0), jnp.concatenate([b1, b2, b1], axis=0), TN)
            for h in range(stop, count):
                tiles[h] = jnp.where(inner, 0.0, tiles[h]) - update[8 * h : 8 * h + 8]
    uppers, inverses = [], []
    for h, tile in enumerate(tiles):
        rows = row_in_tile + 8 * h
        over = jnp.sqrt(every[h])
        uppers.append(jnp.where(lanes > rows, tile * over, jnp.where(lanes == rows, 1.0 / over, 0.0)))
        inverses.append(jnp.where(lanes < rows, tile * over, jnp.where(lanes == rows, over, 0.0)))
    return uppers, inverses


def plane_peers(sizes, gx, gy):
    nx, ny, _ = sizes
    cores = 2 if ny % 2 == 0 else 1
    chips = ny // cores
    for dx in range(nx - 1, -1, -1):
        for dy in range(chips - 1, -1, -1):
            for core in range(cores):
                if (dx, dy, core) != (0, 0, 0):
                    chip = lax.rem(gy // cores + dy, chips)
                    yield lax.rem(gx + dx, nx), chip * cores + lax.rem(lax.rem(gy, cores) + core, cores)


def greet(sizes):
    nx, ny, nz = sizes
    gx, gy, gz = lax.axis_index("gx"), lax.axis_index("gy"), lax.axis_index("gz")
    barrier = pltpu.get_barrier_semaphore()
    for px, py in plane_peers(sizes, gx, gy):
        pl.semaphore_signal(barrier, inc=1, device_id=(px, py, gz), device_id_type=MESH)
    for step in range(1, nz):
        pl.semaphore_signal(barrier, inc=1, device_id=(gx, gy, lax.rem(gz + step, nz)), device_id_type=MESH)


class Exchange:
    def __init__(self, sizes, send, landed, column, gathered, send_sem, recv_sem):
        nx, ny, nz = sizes
        self.nz, self.group = nz, nx * ny
        self.send, self.landed, self.column, self.gathered = send, landed, column, gathered
        self.send_sem, self.recv_sem = send_sem, recv_sem
        gx, gy, gz = lax.axis_index("gx"), lax.axis_index("gy"), lax.axis_index("gz")
        self.me, self.gz = gx * ny + gy, gz
        me = self.me

        def copy(src, dst, at, device):
            return pltpu.make_async_remote_copy(
                src_ref=src, dst_ref=dst, send_sem=send_sem.at[at], recv_sem=recv_sem.at[at], device_id=device, device_id_type=MESH
            )

        self.out, self.back = [], []
        for slot, (px, py) in enumerate(plane_peers(sizes, gx, gy)):
            self.out.append(copy(send.at[px * ny + py], landed.at[slot], 0, (px, py, gz)))
            self.back.append(copy(gathered.at[me], gathered.at[me], 2, (px, py, gz)))
        self.along = [copy(column.at[gz], column.at[gz], 1, (gx, gy, lax.rem(gz + step, nz))) for step in range(nz - 1, 0, -1)]

    def wait(self, ref, sem):
        pltpu.make_async_copy(ref, ref, sem).wait()

    def parts(self):
        self.wait(self.landed, self.recv_sem.at[0])
        yield self.send[self.me]
        for slot in range(self.group - 1):
            yield self.landed[slot]

    def columns(self):
        self.wait(self.column.at[pl.ds(0, self.nz - 1)], self.recv_sem.at[1])
        for z in range(self.nz):
            yield self.column[z]

    def finish(self):
        self.wait(self.gathered.at[pl.ds(0, self.group - 1)], self.recv_sem.at[2])

    def drain(self):
        self.wait(self.landed, self.send_sem.at[0])
        self.wait(self.column.at[pl.ds(0, self.nz - 1)], self.send_sem.at[1])
        self.wait(self.gathered.at[pl.ds(0, self.group - 1)], self.send_sem.at[2])


def start(copies):
    for copy in copies:
        copy.start()


def sum_pairs(values):
    total, lost = None, None
    for value in values:
        if total is None:
            total = value
        else:
            total, off = two_sum(total, value)
            lost = off if lost is None else lost + off
    return total, jnp.zeros_like(total) if lost is None else lost


def sum_plain(values):
    total = None
    for value in values:
        total = value if total is None else total + value
    return total


def exchange_scratch(sizes, rows, size):
    nx, ny, nz = sizes
    group = nx * ny
    return [
        pltpu.VMEM((group, rows, size), jnp.float32),
        pltpu.VMEM((group - 1, rows, size), jnp.float32),
        pltpu.VMEM((nz, rows, size), jnp.float32),
        pltpu.VMEM((group, rows, size), jnp.float32),
        pltpu.SemaphoreType.DMA((3,)),
        pltpu.SemaphoreType.DMA((3,)),
    ]


def halves(span):
    middle = (span.start + span.stop) // 2
    return slice(span.start, middle), slice(middle, span.stop)


def chunk_of(width, most):
    return most if width % most == 0 else width


def reduce_kernel(sizes, panel, trailing, gram_out, rest_out, off_out, product_out, inverse_out, pieces, trailing_held, panel_held, move_sem, *scratch):
    size, width = panel.shape
    trail = trailing.shape[0]
    group = sizes[0] * sizes[1]
    rows, less = size // group, trail // group
    chunk = chunk_of(width, 1024)
    steps = width // chunk
    sliced = scratch[12:]
    spans = [slice(i * chunk, (i + 1) * chunk) for i in range(steps)]
    loads = []
    for i in range(steps):
        at = pl.ds(i * chunk, chunk)
        loads.append(pltpu.make_async_copy(panel.at[:, at], panel_held.at[:, at], move_sem.at[i]))
    loads.append(pltpu.make_async_copy(trailing, trailing_held, move_sem.at[steps]))
    start(loads)
    greet(sizes)
    none = lax.axis_index("gx") // sizes[0]
    zero = jnp.zeros((size, size), jnp.float32)
    gram, lost, small = zero, zero, zero
    for i in range(steps + 1):
        if i < steps:
            loads[i].wait()
            for t in range(0, size, 16):
                for place, part in enumerate(slices(panel_held[t : t + 16, spans[i]])):
                    sliced[i][0, place * size + t : place * size + t + 16] = part.astype(jnp.bfloat16)
        if i > 0:
            for half in halves(slice(0, chunk)):
                pair = sliced[i - 1][none, :, half]
                found = dot(pair, pair, NT)
                gram, off = two_sum(gram, found[:size, :size])
                lost = lost + off
                small = small + ((found[:size, size:] + found[size:, :size]) + found[size:, size:])
    gram, off = two_sum(gram, small)
    lost = lost + off
    heads = Exchange(sizes, *scratch[:6])
    tails = Exchange(sizes, *scratch[6:12])
    for p in range(group):
        heads.send[p] = gram[p * rows : (p + 1) * rows]
    pl.semaphore_wait(pltpu.get_barrier_semaphore(), group - 1 + sizes[2] - 1)
    start(heads.out)
    loads[steps].wait()
    cross = jnp.zeros((trail, size), jnp.float32)
    lows = zero
    for i, span in enumerate(spans):
        pair = sliced[i][none]
        low = (panel_held[:, span] - pair[:size].astype(jnp.float32)) - pair[size:].astype(jnp.float32)
        low = low.astype(jnp.bfloat16)
        one, two = terms(trailing_held[:, span], 2)
        left = jnp.concatenate([low, one, two], axis=0)
        found = dot(left, pair, NT)
        last = dot(left, low, NT)
        found = found[:, :size] + found[:, size:]
        lows = lows + found[:size]
        lost = lost + last[:size]
        found = found[size:] + last[size:]
        cross = cross + (found[:trail] + found[trail:])
    lost = lost + (lows + lows.T)
    for p in range(group):
        tails.send[p, :rows] = lost[p * rows : (p + 1) * rows]
        tails.send[p, rows:] = cross[p * less : (p + 1) * less]
    start(tails.out)
    for span in spans:
        for t in range(0, size, 16):
            for place, term in enumerate(terms(panel_held[t : t + 16, span], 3)):
                pieces[place * size + t : place * size + t + 16, span] = term
    total, lost_out = sum_pairs(heads.parts())
    heads.column[heads.gz] = total
    start(heads.along)
    part = sum_plain(tails.parts())
    tails.column[tails.gz, :rows] = part[:rows] + lost_out
    tails.column[tails.gz, rows:] = part[rows:]
    start(tails.along)
    total, lost_along = sum_pairs(heads.columns())
    heads.gathered[heads.me] = total
    start(heads.back)
    part = sum_plain(tails.columns())
    tails.gathered[tails.me, :rows] = part[:rows] + lost_along
    tails.gathered[tails.me, rows:] = part[rows:]
    start(tails.back)
    heads.finish()
    gram = jnp.concatenate([heads.gathered[p] for p in range(group)], axis=0)
    uppers, inverses = factor([gram[h : h + 8] for h in range(0, size, 8)])
    inverse = jnp.concatenate(inverses, axis=0)
    gram_out[...] = gram
    inverse_out[...] = inverse
    off, turned = departure(gram, jnp.concatenate(uppers, axis=0), inverse)
    off_out[...] = off
    product_out[...] = turned
    tails.finish()
    for p in range(group):
        rest_out[p] = tails.gathered[p]
    heads.drain()
    tails.drain()


def departure(gram, upper, inverse):
    size = gram.shape[0]
    lower = upper.T
    high, middle = slices(lower)
    low = ((lower - high) - middle).astype(jnp.bfloat16)
    pair = narrow(high, middle)
    first = dot(pair, pair, NT)
    second = dot(low, pair, NT)
    mixed = first[:size, size:] + (second[:, :size] + second[:, size:])
    small = (first[size:, size:] + dot(low, low, NT)) + (mixed + mixed.T)
    off, lower_off = two_sum(gram, -first[:size, :size])
    lower = (high + middle) + low.astype(jnp.float32)
    return (off - small) + lower_off, product(inverse, lower, NN)


def refine(off, turned, inverse):
    size = off.shape[0]
    row = lax.broadcasted_iota(jnp.int32, (size, size), 0)
    lane = lax.broadcasted_iota(jnp.int32, (size, size), 1)
    moved = close_product(inverse, off, NN)
    second_gram = close_product(turned, turned, NT) + close_product(moved, inverse, NT)
    step = jnp.where(row > lane, second_gram, jnp.where(row == lane, 0.5 * second_gram - 0.5, 0.0))
    rough = step.astype(jnp.bfloat16)
    square = dot(rough, rough, NN)
    twice = dot(rough, rough, NT)
    return (square + jnp.where(row > lane, twice, jnp.where(row == lane, 0.5 * twice, 0.0))) - step


def final_kernel(scale, gram, rest, off, turned, inverse, pieces, trailing, basis, upper, coupling, updated, basis_held, updated_held, upper_held, coupling_held, store_sem):
    size, width = basis.shape
    chunk = chunk_of(width, 512)
    steps = width // chunk
    group = rest.shape[0]
    rows = size // group
    lost = jnp.concatenate([rest[p, :rows] for p in range(group)], axis=0)
    cross = jnp.concatenate([rest[p, rows:] for p in range(group)], axis=0)
    inverse = inverse[...]
    mixed = product(cross, inverse, NT)
    change = refine(off[...] + lost, turned[...], inverse)
    whole = inverse + product(change, inverse, NN)
    mixed = mixed + close_product(mixed, change, NT)
    coupling_held[...] = mixed
    left = left_terms(jnp.concatenate([whole * scale, product(mixed, whole, NN)], axis=0))
    stores = []

    def store(src, dst, place):
        stores.append(pltpu.make_async_copy(src, dst, store_sem.at[place]))
        stores[-1].start()

    for i in range(steps):
        span, at = slice(i * chunk, (i + 1) * chunk), pl.ds(i * chunk, chunk)
        one, two, three = (pieces[t * size : (t + 1) * size, span] for t in range(3))
        right = jnp.concatenate([one, three, two, one, two, one], axis=0)
        out = dot(left, right, NN)
        basis_held[:, span] = out[:size]
        store(basis_held.at[:, at], basis.at[:, at], 2 * i)
        projected = out[size:]
        updated_held[:, span] = trailing[:, span] - projected
        store(updated_held.at[:, at], updated.at[:, at], 2 * i + 1)
        if i == steps - 1:
            row = lax.broadcasted_iota(jnp.int32, (size, size), 0)
            lane = lax.broadcasted_iota(jnp.int32, (size, size), 1)
            total = product(whole, gram[...], NN) + dot(whole.astype(jnp.bfloat16), lost.astype(jnp.bfloat16), NN)
            upper_held[...] = jnp.where(row <= lane, total * (1.0 / scale), 0.0)
            store(coupling_held, coupling, 2 * steps)
            store(upper_held, upper, 2 * steps + 1)
    for copy in stores:
        copy.wait()


def shards(sizes, panel, trailing):
    size, width = panel.shape
    trail = trailing.shape[0]
    nx, ny, nz = sizes
    group = nx * ny
    rows, less = size // group, trail // group
    f32 = jnp.float32
    scale = float(width * group * nz) ** 0.5

    def params(identity=None, mebibytes=40):
        return pltpu.CompilerParams(
            collective_id=identity, has_side_effects=identity is not None, vmem_limit_bytes=mebibytes * 2**20
        )

    square = jax.ShapeDtypeStruct((size, size), f32)
    held = pl.pallas_call(
        functools.partial(reduce_kernel, sizes),
        out_shape=[
            square,
            jax.ShapeDtypeStruct((group, rows + less, size), f32),
            square,
            square,
            square,
            jax.ShapeDtypeStruct((3 * size, width), jnp.bfloat16),
            jax.ShapeDtypeStruct((trail, width), f32),
        ],
        in_specs=[HBM, HBM],
        out_specs=[VMEM] * 7,
        scratch_shapes=[
            pltpu.VMEM((size, width), f32),
            pltpu.SemaphoreType.DMA((width // chunk_of(width, 1024) + 1,)),
            *exchange_scratch(sizes, rows, size),
            *exchange_scratch(sizes, rows + less, size),
            *[pltpu.VMEM((1, 2 * size, chunk_of(width, 1024)), jnp.bfloat16) for _ in range(width // chunk_of(width, 1024))],
        ],
        compiler_params=params(0),
        name="reduce",
    )(pltpu.with_memory_space_constraint(panel, pltpu.HBM), pltpu.with_memory_space_constraint(trailing, pltpu.HBM))
    basis, upper, coupling_t, updated = pl.pallas_call(
        functools.partial(final_kernel, scale),
        out_shape=[
            jax.ShapeDtypeStruct((size, width), f32),
            square,
            jax.ShapeDtypeStruct((trail, size), f32),
            jax.ShapeDtypeStruct((trail, width), f32),
        ],
        in_specs=[VMEM] * 7,
        out_specs=[HBM] * 4,
        scratch_shapes=[
            pltpu.VMEM((size, width), f32),
            pltpu.VMEM((trail, width), f32),
            pltpu.VMEM((size, size), f32),
            pltpu.VMEM((trail, size), f32),
            pltpu.SemaphoreType.DMA((2 * (width // chunk_of(width, 512)) + 2,)),
        ],
        compiler_params=params(),
        name="final",
    )(*held)
    return basis, upper, coupling_t.T, updated


def solution(mesh):
    sizes = tuple(mesh.shape[name] for name in ("gx", "gy", "gz"))
    placed = P(None, ("gx", "gy", "gz"))
    return jax.shard_map(
        functools.partial(shards, sizes),
        mesh=mesh,
        in_specs=(placed, placed),
        out_specs=(placed, P(), P(), placed),
        check_vma=False,
    )
```

```python
import functools

import jax
import jax.numpy as jnp
from jax import lax
from jax.experimental import pallas as pl
from jax.experimental.pallas import tpu as pltpu
from jax.sharding import PartitionSpec as P

MESH = pl.DeviceIdType.MESH
NT = (((1,), (1,)), ((), ()))
NN = (((1,), (0,)), ((), ()))
TN = (((0,), (0,)), ((), ()))
VMEM = pl.BlockSpec(memory_space=pltpu.VMEM)
HBM = pl.BlockSpec(memory_space=pltpu.HBM)


def dot(left, right, dims):
    return lax.dot_general(left, right, dims, preferred_element_type=jnp.float32)


def terms(value, count):
    found = []
    for _ in range(count):
        term = value.astype(jnp.bfloat16)
        found.append(term)
        value = value - term.astype(jnp.float32)
    return found


def left_terms(value):
    one, two, three = terms(value, 3)
    return jnp.concatenate([three, one, two, two, one, one], axis=1)


def right_terms(value, axis):
    one, two, three = terms(value, 3)
    return jnp.concatenate([one, three, two, one, two, one], axis=axis)


def product(left, right, dims):
    return dot(left_terms(left), right_terms(right, 1 if dims is NT else 0), dims)


def close_product(left, right, dims):
    one, two = terms(left, 2)
    first, second = terms(right, 2)
    axis = 1 if dims is NT else 0
    return dot(jnp.concatenate([two, one, one], axis=1), jnp.concatenate([first, second, first], axis=axis), dims)


def slices(value):
    top = jnp.max(jnp.abs(value), axis=1, keepdims=True) * 2.0**17
    high = (value + top) - top
    rest = value - high
    top = top * 2.0**-9
    return high, (rest + top) - top


def narrow(*values):
    return jnp.concatenate([value.astype(jnp.bfloat16) for value in values], axis=0)


def two_sum(one, two):
    total = one + two
    added = total - one
    return total, (one - (total - added)) + (two - added)


def factor(tiles, depth=8):
    size = tiles[0].shape[1]
    shape = (8, size)
    lanes = lax.broadcasted_iota(jnp.int32, shape, 1)
    row_in_tile = lax.broadcasted_iota(jnp.int32, shape, 0)
    tiles = list(tiles)
    count = len(tiles)
    every = []

    def across(tile, column):
        return jnp.broadcast_to(jnp.sum(jnp.where(lanes == column, tile, 0.0), axis=1, keepdims=True), shape)

    def down(tile, row):
        return jnp.broadcast_to(tile[row : row + 1, :], shape)

    for start in range(0, count, depth):
        stop = min(start + depth, count)
        own = [across(tiles[start], 8 * start + j) for j in range(8)]
        scales = []
        for at in range(start, stop):
            first = 8 * at
            inside = (lanes >= first) & (lanes < first + 8)
            raw = list(tiles)
            columns = after = None
            if at + 1 < stop:
                columns = [across(raw[at + 1], first + j) for j in range(8)]
                after = [across(raw[at + 1], first + 8 + j) for j in range(8)]
            tile = tiles[at]
            scaled, ratios, scale = [], [], None
            for h in range(at + 1, stop):
                tiles[h] = jnp.where(inside, 0.0, tiles[h])
            for r in range(8):
                k = first + r
                pivots = {j: down(own[j], r) for j in range(r, 8)}
                over = 1.0 / pivots[r]
                scale = over if scale is None else jnp.where(row_in_tile == r, over, scale)
                ratios.append({j: pivots[j] * over for j in range(r + 1, 8)})
                unit = jnp.where(lanes == k, 1.0, down(tile, r))
                scaled.append(jnp.where(inside & (lanes > k), 0.0, unit) * over)
                if r < 7:
                    for j in range(r + 1, 8):
                        own[j] = own[j] - own[r] * ratios[r][j]
                    below = jnp.where(lanes == k, 0.0, tile) - (own[r] * over) * unit
                    tile = jnp.where(row_in_tile > r, below, tile)
                if after is not None:
                    column = columns[r]
                    for j in range(r + 1, 8):
                        columns[j] = columns[j] - column * ratios[r][j]
                    tiles[at + 1] = tiles[at + 1] - column * scaled[r]
                    times = column * over
                    for j in range(8):
                        after[j] = after[j] - times * down(column, j)
            tiles[at] = tile
            scales.append(scale)
            every.append(scale)
            for h in range(at + 2, stop):
                columns = [across(raw[h], first + j) for j in range(8)]
                total = tiles[h]
                for r in range(8):
                    column = columns[r]
                    for j in range(r + 1, 8):
                        columns[j] = columns[j] - column * ratios[r][j]
                    total = total - column * scaled[r]
                tiles[h] = total
            own = after
        if stop < count:
            inner = (lanes >= 8 * start) & (lanes < 8 * stop)
            left = jnp.concatenate(tiles[start:stop], axis=0)
            right = []
            for h in range(start, stop):
                rows = row_in_tile + 8 * h
                right.append(jnp.where(lanes == rows, 1.0, jnp.where(inner & (lanes > rows), 0.0, tiles[h])) * scales[h - start])
            b1, b2, b3 = terms(jnp.concatenate(right, axis=0), 3)
            a1, a2, a3 = terms(left, 3)
            update = dot(jnp.concatenate([a3, a1, a2], axis=0), jnp.concatenate([b1, b3, b2], axis=0), TN)
            update = update + dot(jnp.concatenate([a2, a1, a1], axis=0), jnp.concatenate([b1, b2, b1], axis=0), TN)
            for h in range(stop, count):
                tiles[h] = jnp.where(inner, 0.0, tiles[h]) - update[8 * h : 8 * h + 8]
    uppers, inverses = [], []
    for h, tile in enumerate(tiles):
        rows = row_in_tile + 8 * h
        over = jnp.sqrt(every[h])
        uppers.append(jnp.where(lanes > rows, tile * over, jnp.where(lanes == rows, 1.0 / over, 0.0)))
        inverses.append(jnp.where(lanes < rows, tile * over, jnp.where(lanes == rows, over, 0.0)))
    return uppers, inverses


def plane_peers(sizes, gx, gy):
    nx, ny, _ = sizes
    cores = 2 if ny % 2 == 0 else 1
    chips = ny // cores
    for dx in range(nx - 1, -1, -1):
        for dy in range(chips - 1, -1, -1):
            for core in range(cores):
                if (dx, dy, core) != (0, 0, 0):
                    chip = lax.rem(gy // cores + dy, chips)
                    yield lax.rem(gx + dx, nx), chip * cores + lax.rem(lax.rem(gy, cores) + core, cores)


def greet(sizes):
    nx, ny, nz = sizes
    gx, gy, gz = lax.axis_index("gx"), lax.axis_index("gy"), lax.axis_index("gz")
    barrier = pltpu.get_barrier_semaphore()
    for px, py in plane_peers(sizes, gx, gy):
        pl.semaphore_signal(barrier, inc=1, device_id=(px, py, gz), device_id_type=MESH)
    for step in range(1, nz):
        pl.semaphore_signal(barrier, inc=1, device_id=(gx, gy, lax.rem(gz + step, nz)), device_id_type=MESH)


class Exchange:
    def __init__(self, sizes, send, landed, column, gathered, send_sem, recv_sem):
        nx, ny, nz = sizes
        self.nz, self.group = nz, nx * ny
        self.send, self.landed, self.column, self.gathered = send, landed, column, gathered
        self.send_sem, self.recv_sem = send_sem, recv_sem
        gx, gy, gz = lax.axis_index("gx"), lax.axis_index("gy"), lax.axis_index("gz")
        self.me, self.gz = gx * ny + gy, gz
        me = self.me

        def copy(src, dst, at, device):
            return pltpu.make_async_remote_copy(
                src_ref=src, dst_ref=dst, send_sem=send_sem.at[at], recv_sem=recv_sem.at[at], device_id=device, device_id_type=MESH
            )

        self.out, self.back = [], []
        for slot, (px, py) in enumerate(plane_peers(sizes, gx, gy)):
            self.out.append(copy(send.at[px * ny + py], landed.at[slot], 0, (px, py, gz)))
            self.back.append(copy(gathered.at[me], gathered.at[me], 2, (px, py, gz)))
        self.along = [copy(column.at[gz], column.at[gz], 1, (gx, gy, lax.rem(gz + step, nz))) for step in range(nz - 1, 0, -1)]

    def wait(self, ref, sem):
        pltpu.make_async_copy(ref, ref, sem).wait()

    def parts(self):
        self.wait(self.landed, self.recv_sem.at[0])
        yield self.send[self.me]
        for slot in range(self.group - 1):
            yield self.landed[slot]

    def columns(self):
        self.wait(self.column.at[pl.ds(0, self.nz - 1)], self.recv_sem.at[1])
        for z in range(self.nz):
            yield self.column[z]

    def finish(self):
        self.wait(self.gathered.at[pl.ds(0, self.group - 1)], self.recv_sem.at[2])

    def drain(self):
        self.wait(self.landed, self.send_sem.at[0])
        self.wait(self.column.at[pl.ds(0, self.nz - 1)], self.send_sem.at[1])
        self.wait(self.gathered.at[pl.ds(0, self.group - 1)], self.send_sem.at[2])


def start(copies):
    for copy in copies:
        copy.start()


def sum_pairs(values):
    total, lost = None, None
    for value in values:
        if total is None:
            total = value
        else:
            total, off = two_sum(total, value)
            lost = off if lost is None else lost + off
    return total, jnp.zeros_like(total) if lost is None else lost


def sum_plain(values):
    total = None
    for value in values:
        total = value if total is None else total + value
    return total


def exchange_scratch(sizes, rows, size):
    nx, ny, nz = sizes
    group = nx * ny
    return [
        pltpu.VMEM((group, rows, size), jnp.float32),
        pltpu.VMEM((group - 1, rows, size), jnp.float32),
        pltpu.VMEM((nz, rows, size), jnp.float32),
        pltpu.VMEM((group, rows, size), jnp.float32),
        pltpu.SemaphoreType.DMA((3,)),
        pltpu.SemaphoreType.DMA((3,)),
    ]


def halves(span):
    middle = (span.start + span.stop) // 2
    return slice(span.start, middle), slice(middle, span.stop)


def chunk_of(width, most):
    return most if width % most == 0 else width


def reduce_kernel(sizes, panel, trailing, gram_out, rest_out, off_out, product_out, inverse_out, pieces, trailing_held, panel_held, move_sem, *scratch):
    size, width = panel.shape
    trail = trailing.shape[0]
    group = sizes[0] * sizes[1]
    rows, less = size // group, trail // group
    chunk = chunk_of(width, 1024)
    steps = width // chunk
    sliced = scratch[12:]
    spans = [slice(i * chunk, (i + 1) * chunk) for i in range(steps)]
    loads = []
    for i in range(steps):
        at = pl.ds(i * chunk, chunk)
        loads.append(pltpu.make_async_copy(panel.at[:, at], panel_held.at[:, at], move_sem.at[i]))
    loads.append(pltpu.make_async_copy(trailing, trailing_held, move_sem.at[steps]))
    start(loads)
    greet(sizes)
    none = lax.axis_index("gx") // sizes[0]
    zero = jnp.zeros((size, size), jnp.float32)
    gram, lost, small = zero, zero, zero
    for i in range(steps + 1):
        if i < steps:
            loads[i].wait()
            for t in range(0, size, 16):
                for place, part in enumerate(slices(panel_held[t : t + 16, spans[i]])):
                    sliced[i][0, place * size + t : place * size + t + 16] = part.astype(jnp.bfloat16)
        if i > 0:
            for half in halves(slice(0, chunk)):
                pair = sliced[i - 1][none, :, half]
                found = dot(pair, pair, NT)
                gram, off = two_sum(gram, found[:size, :size])
                lost = lost + off
                small = small + ((found[:size, size:] + found[size:, :size]) + found[size:, size:])
    gram, off = two_sum(gram, small)
    lost = lost + off
    heads = Exchange(sizes, *scratch[:6])
    tails = Exchange(sizes, *scratch[6:12])
    for p in range(group):
        heads.send[p] = gram[p * rows : (p + 1) * rows]
    pl.semaphore_wait(pltpu.get_barrier_semaphore(), group - 1 + sizes[2] - 1)
    start(heads.out)
    loads[steps].wait()
    cross = jnp.zeros((trail, size), jnp.float32)
    lows = zero
    for i, span in enumerate(spans):
        pair = sliced[i][none]
        low = (panel_held[:, span] - pair[:size].astype(jnp.float32)) - pair[size:].astype(jnp.float32)
        low = low.astype(jnp.bfloat16)
        one, two = terms(trailing_held[:, span], 2)
        left = jnp.concatenate([low, one, two], axis=0)
        found = dot(left, pair, NT)
        last = dot(left, low, NT)
        found = found[:, :size] + found[:, size:]
        lows = lows + found[:size]
        lost = lost + last[:size]
        found = found[size:] + last[size:]
        cross = cross + (found[:trail] + found[trail:])
    lost = lost + (lows + lows.T)
    for p in range(group):
        tails.send[p, :rows] = lost[p * rows : (p + 1) * rows]
        tails.send[p, rows:] = cross[p * less : (p + 1) * less]
    for span in spans:
        for t in range(0, size, 16):
            for place, term in enumerate(terms(panel_held[t : t + 16, span], 3)):
                pieces[place * size + t : place * size + t + 16, span] = term
    start(tails.out)
    total, lost_out = sum_pairs(heads.parts())
    heads.column[heads.gz] = total
    start(heads.along)
    part = sum_plain(tails.parts())
    tails.column[tails.gz, :rows] = part[:rows] + lost_out
    tails.column[tails.gz, rows:] = part[rows:]
    start(tails.along)
    total, lost_along = sum_pairs(heads.columns())
    heads.gathered[heads.me] = total
    start(heads.back)
    part = sum_plain(tails.columns())
    tails.gathered[tails.me, :rows] = part[:rows] + lost_along
    tails.gathered[tails.me, rows:] = part[rows:]
    start(tails.back)
    heads.finish()
    gram = jnp.concatenate([heads.gathered[p] for p in range(group)], axis=0)
    uppers, inverses = factor([gram[h : h + 8] for h in range(0, size, 8)])
    inverse = jnp.concatenate(inverses, axis=0)
    gram_out[...] = gram
    inverse_out[...] = inverse
    off, turned = departure(gram, jnp.concatenate(uppers, axis=0), inverse)
    off_out[...] = off
    product_out[...] = turned
    tails.finish()
    for p in range(group):
        rest_out[p] = tails.gathered[p]
    heads.drain()
    tails.drain()


def departure(gram, upper, inverse):
    size = gram.shape[0]
    lower = upper.T
    high, middle = slices(lower)
    low = ((lower - high) - middle).astype(jnp.bfloat16)
    pair = narrow(high, middle)
    first = dot(pair, pair, NT)
    second = dot(low, pair, NT)
    mixed = first[:size, size:] + (second[:, :size] + second[:, size:])
    small = (first[size:, size:] + dot(low, low, NT)) + (mixed + mixed.T)
    off, lower_off = two_sum(gram, -first[:size, :size])
    lower = (high + middle) + low.astype(jnp.float32)
    return (off - small) + lower_off, product(inverse, lower, NN)


def refine(off, turned, inverse):
    size = off.shape[0]
    row = lax.broadcasted_iota(jnp.int32, (size, size), 0)
    lane = lax.broadcasted_iota(jnp.int32, (size, size), 1)
    moved = close_product(inverse, off, NN)
    second_gram = close_product(turned, turned, NT) + close_product(moved, inverse, NT)
    step = jnp.where(row > lane, second_gram, jnp.where(row == lane, 0.5 * second_gram - 0.5, 0.0))
    rough = step.astype(jnp.bfloat16)
    square = dot(rough, rough, NN)
    twice = dot(rough, rough, NT)
    return (square + jnp.where(row > lane, twice, jnp.where(row == lane, 0.5 * twice, 0.0))) - step


def final_kernel(scale, gram, rest, off, turned, inverse, pieces, trailing, basis, upper, coupling, updated, basis_held, updated_held, upper_held, coupling_held, store_sem):
    size, width = basis.shape
    chunk = chunk_of(width, 512)
    steps = width // chunk
    group = rest.shape[0]
    rows = size // group
    lost = jnp.concatenate([rest[p, :rows] for p in range(group)], axis=0)
    cross = jnp.concatenate([rest[p, rows:] for p in range(group)], axis=0)
    inverse = inverse[...]
    mixed = product(cross, inverse, NT)
    change = refine(off[...] + lost, turned[...], inverse)
    whole = inverse + product(change, inverse, NN)
    mixed = mixed + close_product(mixed, change, NT)
    coupling_held[...] = mixed
    left = left_terms(jnp.concatenate([whole * scale, product(mixed, whole, NN)], axis=0))
    stores = []

    def store(src, dst, place):
        stores.append(pltpu.make_async_copy(src, dst, store_sem.at[place]))
        stores[-1].start()

    for i in range(steps):
        span, at = slice(i * chunk, (i + 1) * chunk), pl.ds(i * chunk, chunk)
        one, two, three = (pieces[t * size : (t + 1) * size, span] for t in range(3))
        right = jnp.concatenate([one, three, two, one, two, one], axis=0)
        out = dot(left, right, NN)
        basis_held[:, span] = out[:size]
        store(basis_held.at[:, at], basis.at[:, at], 2 * i)
        projected = out[size:]
        updated_held[:, span] = trailing[:, span] - projected
        store(updated_held.at[:, at], updated.at[:, at], 2 * i + 1)
        if i == steps - 1:
            row = lax.broadcasted_iota(jnp.int32, (size, size), 0)
            lane = lax.broadcasted_iota(jnp.int32, (size, size), 1)
            total = product(whole, gram[...], NN) + dot(whole.astype(jnp.bfloat16), lost.astype(jnp.bfloat16), NN)
            upper_held[...] = jnp.where(row <= lane, total * (1.0 / scale), 0.0)
            store(coupling_held, coupling, 2 * steps)
            store(upper_held, upper, 2 * steps + 1)
    for copy in stores:
        copy.wait()


def shards(sizes, panel, trailing):
    size, width = panel.shape
    trail = trailing.shape[0]
    nx, ny, nz = sizes
    group = nx * ny
    rows, less = size // group, trail // group
    f32 = jnp.float32
    scale = float(width * group * nz) ** 0.5

    def params(identity=None, mebibytes=40):
        return pltpu.CompilerParams(
            collective_id=identity, has_side_effects=identity is not None, vmem_limit_bytes=mebibytes * 2**20
        )

    square = jax.ShapeDtypeStruct((size, size), f32)
    held = pl.pallas_call(
        functools.partial(reduce_kernel, sizes),
        out_shape=[
            square,
            jax.ShapeDtypeStruct((group, rows + less, size), f32),
            square,
            square,
            square,
            jax.ShapeDtypeStruct((3 * size, width), jnp.bfloat16),
            jax.ShapeDtypeStruct((trail, width), f32),
        ],
        in_specs=[HBM, HBM],
        out_specs=[VMEM] * 7,
        scratch_shapes=[
            pltpu.VMEM((size, width), f32),
            pltpu.SemaphoreType.DMA((width // chunk_of(width, 1024) + 1,)),
            *exchange_scratch(sizes, rows, size),
            *exchange_scratch(sizes, rows + less, size),
            *[pltpu.VMEM((1, 2 * size, chunk_of(width, 1024)), jnp.bfloat16) for _ in range(width // chunk_of(width, 1024))],
        ],
        compiler_params=params(0),
        name="reduce",
    )(pltpu.with_memory_space_constraint(panel, pltpu.HBM), pltpu.with_memory_space_constraint(trailing, pltpu.HBM))
    basis, upper, coupling_t, updated = pl.pallas_call(
        functools.partial(final_kernel, scale),
        out_shape=[
            jax.ShapeDtypeStruct((size, width), f32),
            square,
            jax.ShapeDtypeStruct((trail, size), f32),
            jax.ShapeDtypeStruct((trail, width), f32),
        ],
        in_specs=[VMEM] * 7,
        out_specs=[HBM] * 4,
        scratch_shapes=[
            pltpu.VMEM((size, width), f32),
            pltpu.VMEM((trail, width), f32),
            pltpu.VMEM((size, size), f32),
            pltpu.VMEM((trail, size), f32),
            pltpu.SemaphoreType.DMA((2 * (width // chunk_of(width, 512)) + 2,)),
        ],
        compiler_params=params(),
        name="final",
    )(*held)
    return basis, upper, coupling_t.T, updated


def solution(mesh):
    sizes = tuple(mesh.shape[name] for name in ("gx", "gy", "gz"))
    placed = P(None, ("gx", "gy", "gz"))
    return jax.shard_map(
        functools.partial(shards, sizes),
        mesh=mesh,
        in_specs=(placed, placed),
        out_specs=(placed, P(), P(), placed),
        check_vma=False,
    )
```

```python
import functools

import jax
import jax.numpy as jnp
from jax import lax
from jax.experimental import pallas as pl
from jax.experimental.pallas import tpu as pltpu
from jax.sharding import PartitionSpec as P

MESH = pl.DeviceIdType.MESH
NT = (((1,), (1,)), ((), ()))
NN = (((1,), (0,)), ((), ()))
TN = (((0,), (0,)), ((), ()))
VMEM = pl.BlockSpec(memory_space=pltpu.VMEM)
HBM = pl.BlockSpec(memory_space=pltpu.HBM)


def dot(left, right, dims):
    return lax.dot_general(left, right, dims, preferred_element_type=jnp.float32)


def terms(value, count):
    found = []
    for _ in range(count):
        term = value.astype(jnp.bfloat16)
        found.append(term)
        value = value - term.astype(jnp.float32)
    return found


def left_terms(value):
    one, two, three = terms(value, 3)
    return jnp.concatenate([three, one, two, two, one, one], axis=1)


def right_terms(value, axis):
    one, two, three = terms(value, 3)
    return jnp.concatenate([one, three, two, one, two, one], axis=axis)


def product(left, right, dims):
    return dot(left_terms(left), right_terms(right, 1 if dims is NT else 0), dims)


def close_product(left, right, dims):
    one, two = terms(left, 2)
    first, second = terms(right, 2)
    axis = 1 if dims is NT else 0
    return dot(jnp.concatenate([two, one, one], axis=1), jnp.concatenate([first, second, first], axis=axis), dims)


def slices(value):
    top = jnp.max(jnp.abs(value), axis=1, keepdims=True) * 2.0**17
    high = (value + top) - top
    rest = value - high
    top = top * 2.0**-9
    return high, (rest + top) - top


def narrow(*values):
    return jnp.concatenate([value.astype(jnp.bfloat16) for value in values], axis=0)


def two_sum(one, two):
    total = one + two
    added = total - one
    return total, (one - (total - added)) + (two - added)


def factor(tiles, depth=8):
    size = tiles[0].shape[1]
    shape = (8, size)
    lanes = lax.broadcasted_iota(jnp.int32, shape, 1)
    row_in_tile = lax.broadcasted_iota(jnp.int32, shape, 0)
    tiles = list(tiles)
    count = len(tiles)
    every = []

    def across(tile, column):
        return jnp.broadcast_to(jnp.sum(jnp.where(lanes == column, tile, 0.0), axis=1, keepdims=True), shape)

    def down(tile, row):
        return jnp.broadcast_to(tile[row : row + 1, :], shape)

    for start in range(0, count, depth):
        stop = min(start + depth, count)
        own = [across(tiles[start], 8 * start + j) for j in range(8)]
        scales = []
        for at in range(start, stop):
            first = 8 * at
            inside = (lanes >= first) & (lanes < first + 8)
            raw = list(tiles)
            columns = after = None
            if at + 1 < stop:
                columns = [across(raw[at + 1], first + j) for j in range(8)]
                after = [across(raw[at + 1], first + 8 + j) for j in range(8)]
            tile = tiles[at]
            scaled, ratios, scale = [], [], None
            for h in range(at + 1, stop):
                tiles[h] = jnp.where(inside, 0.0, tiles[h])
            for r in range(8):
                k = first + r
                pivots = {j: down(own[j], r) for j in range(r, 8)}
                over = 1.0 / pivots[r]
                scale = over if scale is None else jnp.where(row_in_tile == r, over, scale)
                ratios.append({j: pivots[j] * over for j in range(r + 1, 8)})
                unit = jnp.where(lanes == k, 1.0, down(tile, r))
                scaled.append(jnp.where(inside & (lanes > k), 0.0, unit) * over)
                if r < 7:
                    for j in range(r + 1, 8):
                        own[j] = own[j] - own[r] * ratios[r][j]
                    below = jnp.where(lanes == k, 0.0, tile) - (own[r] * over) * unit
                    tile = jnp.where(row_in_tile > r, below, tile)
                if after is not None:
                    column = columns[r]
                    for j in range(r + 1, 8):
                        columns[j] = columns[j] - column * ratios[r][j]
                    tiles[at + 1] = tiles[at + 1] - column * scaled[r]
                    times = column * over
                    for j in range(8):
                        after[j] = after[j] - times * down(column, j)
            tiles[at] = tile
            scales.append(scale)
            every.append(scale)
            for h in range(at + 2, stop):
                columns = [across(raw[h], first + j) for j in range(8)]
                total = tiles[h]
                for r in range(8):
                    column = columns[r]
                    for j in range(r + 1, 8):
                        columns[j] = columns[j] - column * ratios[r][j]
                    total = total - column * scaled[r]
                tiles[h] = total
            own = after
        if stop < count:
            inner = (lanes >= 8 * start) & (lanes < 8 * stop)
            left = jnp.concatenate(tiles[start:stop], axis=0)
            right = []
            for h in range(start, stop):
                rows = row_in_tile + 8 * h
                right.append(jnp.where(lanes == rows, 1.0, jnp.where(inner & (lanes > rows), 0.0, tiles[h])) * scales[h - start])
            b1, b2, b3 = terms(jnp.concatenate(right, axis=0), 3)
            a1, a2, a3 = terms(left, 3)
            update = dot(jnp.concatenate([a3, a1, a2], axis=0), jnp.concatenate([b1, b3, b2], axis=0), TN)
            update = update + dot(jnp.concatenate([a2, a1, a1], axis=0), jnp.concatenate([b1, b2, b1], axis=0), TN)
            for h in range(stop, count):
                tiles[h] = jnp.where(inner, 0.0, tiles[h]) - update[8 * h : 8 * h + 8]
    uppers, inverses = [], []
    for h, tile in enumerate(tiles):
        rows = row_in_tile + 8 * h
        over = jnp.sqrt(every[h])
        uppers.append(jnp.where(lanes > rows, tile * over, jnp.where(lanes == rows, 1.0 / over, 0.0)))
        inverses.append(jnp.where(lanes < rows, tile * over, jnp.where(lanes == rows, over, 0.0)))
    return uppers, inverses


def plane_peers(sizes, gx, gy):
    nx, ny, _ = sizes
    cores = 2 if ny % 2 == 0 else 1
    chips = ny // cores
    for dx in range(nx - 1, -1, -1):
        for dy in range(chips - 1, -1, -1):
            for core in range(cores):
                if (dx, dy, core) != (0, 0, 0):
                    chip = lax.rem(gy // cores + dy, chips)
                    yield lax.rem(gx + dx, nx), chip * cores + lax.rem(lax.rem(gy, cores) + core, cores)


def greet(sizes):
    nx, ny, nz = sizes
    gx, gy, gz = lax.axis_index("gx"), lax.axis_index("gy"), lax.axis_index("gz")
    barrier = pltpu.get_barrier_semaphore()
    for px, py in plane_peers(sizes, gx, gy):
        pl.semaphore_signal(barrier, inc=1, device_id=(px, py, gz), device_id_type=MESH)
    for step in range(1, nz):
        pl.semaphore_signal(barrier, inc=1, device_id=(gx, gy, lax.rem(gz + step, nz)), device_id_type=MESH)


class Exchange:
    def __init__(self, sizes, send, landed, column, gathered, send_sem, recv_sem):
        nx, ny, nz = sizes
        self.nz, self.group = nz, nx * ny
        self.send, self.landed, self.column, self.gathered = send, landed, column, gathered
        self.send_sem, self.recv_sem = send_sem, recv_sem
        gx, gy, gz = lax.axis_index("gx"), lax.axis_index("gy"), lax.axis_index("gz")
        self.me, self.gz = gx * ny + gy, gz
        me = self.me

        def copy(src, dst, at, device):
            return pltpu.make_async_remote_copy(
                src_ref=src, dst_ref=dst, send_sem=send_sem.at[at], recv_sem=recv_sem.at[at], device_id=device, device_id_type=MESH
            )

        self.out, self.back = [], []
        for slot, (px, py) in enumerate(plane_peers(sizes, gx, gy)):
            self.out.append(copy(send.at[px * ny + py], landed.at[slot], 0, (px, py, gz)))
            self.back.append(copy(gathered.at[me], gathered.at[me], 2, (px, py, gz)))
        self.along = [copy(column.at[gz], column.at[gz], 1, (gx, gy, lax.rem(gz + step, nz))) for step in range(nz - 1, 0, -1)]

    def wait(self, ref, sem):
        pltpu.make_async_copy(ref, ref, sem).wait()

    def parts(self):
        self.wait(self.landed, self.recv_sem.at[0])
        yield self.send[self.me]
        for slot in range(self.group - 1):
            yield self.landed[slot]

    def columns(self):
        self.wait(self.column.at[pl.ds(0, self.nz - 1)], self.recv_sem.at[1])
        for z in range(self.nz):
            yield self.column[z]

    def finish(self):
        self.wait(self.gathered.at[pl.ds(0, self.group - 1)], self.recv_sem.at[2])

    def drain(self):
        self.wait(self.landed, self.send_sem.at[0])
        self.wait(self.column.at[pl.ds(0, self.nz - 1)], self.send_sem.at[1])
        self.wait(self.gathered.at[pl.ds(0, self.group - 1)], self.send_sem.at[2])


def start(copies):
    for copy in copies:
        copy.start()


def sum_pairs(values):
    total, lost = None, None
    for value in values:
        if total is None:
            total = value
        else:
            total, off = two_sum(total, value)
            lost = off if lost is None else lost + off
    return total, jnp.zeros_like(total) if lost is None else lost


def sum_plain(values):
    total = None
    for value in values:
        total = value if total is None else total + value
    return total


def exchange_scratch(sizes, rows, size):
    nx, ny, nz = sizes
    group = nx * ny
    return [
        pltpu.VMEM((group, rows, size), jnp.float32),
        pltpu.VMEM((group - 1, rows, size), jnp.float32),
        pltpu.VMEM((nz, rows, size), jnp.float32),
        pltpu.VMEM((group, rows, size), jnp.float32),
        pltpu.SemaphoreType.DMA((3,)),
        pltpu.SemaphoreType.DMA((3,)),
    ]


def halves(span):
    middle = (span.start + span.stop) // 2
    return slice(span.start, middle), slice(middle, span.stop)


def chunk_of(width, most):
    return most if width % most == 0 else width


def spans_of(width):
    wide, thin = 1024, 512
    if width % wide:
        return [slice(0, width)]
    edges = [0, thin, *range(wide, width + 1, wide)]
    return [slice(low, high) for low, high in zip(edges[:-1], edges[1:])]


def reduce_kernel(sizes, panel, trailing, gram_out, rest_out, off_out, product_out, inverse_out, pieces, trailing_held, panel_held, move_sem, *scratch):
    size, width = panel.shape
    trail = trailing.shape[0]
    group = sizes[0] * sizes[1]
    rows, less = size // group, trail // group
    spans = spans_of(width)
    steps = len(spans)
    sliced = scratch[12:]
    loads = []
    for i, span in enumerate(spans):
        at = pl.ds(span.start, span.stop - span.start)
        loads.append(pltpu.make_async_copy(panel.at[:, at], panel_held.at[:, at], move_sem.at[i]))
    loads.append(pltpu.make_async_copy(trailing, trailing_held, move_sem.at[steps]))
    start(loads)
    greet(sizes)
    none = lax.axis_index("gx") // sizes[0]
    zero = jnp.zeros((size, size), jnp.float32)
    gram, lost, small = zero, zero, zero
    for i in range(steps + 1):
        if i < steps:
            loads[i].wait()
            for t in range(0, size, 16):
                for place, part in enumerate(slices(panel_held[t : t + 16, spans[i]])):
                    sliced[i][0, place * size + t : place * size + t + 16] = part.astype(jnp.bfloat16)
        if i > 0:
            for half in halves(slice(0, spans[i - 1].stop - spans[i - 1].start)):
                pair = sliced[i - 1][none, :, half]
                found = dot(pair, pair, NT)
                gram, off = two_sum(gram, found[:size, :size])
                lost = lost + off
                small = small + ((found[:size, size:] + found[size:, :size]) + found[size:, size:])
    gram, off = two_sum(gram, small)
    lost = lost + off
    heads = Exchange(sizes, *scratch[:6])
    tails = Exchange(sizes, *scratch[6:12])
    for p in range(group):
        heads.send[p] = gram[p * rows : (p + 1) * rows]
    pl.semaphore_wait(pltpu.get_barrier_semaphore(), group - 1 + sizes[2] - 1)
    start(heads.out)
    loads[steps].wait()
    cross = jnp.zeros((trail, size), jnp.float32)
    lows = zero
    for i, span in enumerate(spans):
        pair = sliced[i][none]
        low = (panel_held[:, span] - pair[:size].astype(jnp.float32)) - pair[size:].astype(jnp.float32)
        low = low.astype(jnp.bfloat16)
        one, two = terms(trailing_held[:, span], 2)
        left = jnp.concatenate([low, one, two], axis=0)
        found = dot(left, pair, NT)
        last = dot(left, low, NT)
        found = found[:, :size] + found[:, size:]
        lows = lows + found[:size]
        lost = lost + last[:size]
        found = found[size:] + last[size:]
        cross = cross + (found[:trail] + found[trail:])
    lost = lost + (lows + lows.T)
    for p in range(group):
        tails.send[p, :rows] = lost[p * rows : (p + 1) * rows]
        tails.send[p, rows:] = cross[p * less : (p + 1) * less]
    for span in spans:
        for t in range(0, size, 16):
            for place, term in enumerate(terms(panel_held[t : t + 16, span], 3)):
                pieces[place * size + t : place * size + t + 16, span] = term
    start(tails.out)
    total, lost_out = sum_pairs(heads.parts())
    heads.column[heads.gz] = total
    start(heads.along)
    part = sum_plain(tails.parts())
    tails.column[tails.gz, :rows] = part[:rows] + lost_out
    tails.column[tails.gz, rows:] = part[rows:]
    start(tails.along)
    total, lost_along = sum_pairs(heads.columns())
    heads.gathered[heads.me] = total
    start(heads.back)
    part = sum_plain(tails.columns())
    tails.gathered[tails.me, :rows] = part[:rows] + lost_along
    tails.gathered[tails.me, rows:] = part[rows:]
    start(tails.back)
    heads.finish()
    gram = jnp.concatenate([heads.gathered[p] for p in range(group)], axis=0)
    uppers, inverses = factor([gram[h : h + 8] for h in range(0, size, 8)])
    inverse = jnp.concatenate(inverses, axis=0)
    gram_out[...] = gram
    inverse_out[...] = inverse
    off, turned = departure(gram, jnp.concatenate(uppers, axis=0), inverse)
    off_out[...] = off
    product_out[...] = turned
    tails.finish()
    for p in range(group):
        rest_out[p] = tails.gathered[p]
    heads.drain()
    tails.drain()


def departure(gram, upper, inverse):
    size = gram.shape[0]
    lower = upper.T
    high, middle = slices(lower)
    low = ((lower - high) - middle).astype(jnp.bfloat16)
    pair = narrow(high, middle)
    first = dot(pair, pair, NT)
    second = dot(low, pair, NT)
    mixed = first[:size, size:] + (second[:, :size] + second[:, size:])
    small = (first[size:, size:] + dot(low, low, NT)) + (mixed + mixed.T)
    off, lower_off = two_sum(gram, -first[:size, :size])
    lower = (high + middle) + low.astype(jnp.float32)
    return (off - small) + lower_off, product(inverse, lower, NN)


def refine(off, turned, inverse):
    size = off.shape[0]
    row = lax.broadcasted_iota(jnp.int32, (size, size), 0)
    lane = lax.broadcasted_iota(jnp.int32, (size, size), 1)
    moved = close_product(inverse, off, NN)
    second_gram = close_product(turned, turned, NT) + close_product(moved, inverse, NT)
    step = jnp.where(row > lane, second_gram, jnp.where(row == lane, 0.5 * second_gram - 0.5, 0.0))
    rough = step.astype(jnp.bfloat16)
    square = dot(rough, rough, NN)
    twice = dot(rough, rough, NT)
    return (square + jnp.where(row > lane, twice, jnp.where(row == lane, 0.5 * twice, 0.0))) - step


def final_kernel(scale, gram, rest, off, turned, inverse, pieces, trailing, basis, upper, coupling, updated, basis_held, updated_held, upper_held, coupling_held, store_sem):
    size, width = basis.shape
    chunk = chunk_of(width, 512)
    steps = width // chunk
    group = rest.shape[0]
    rows = size // group
    lost = jnp.concatenate([rest[p, :rows] for p in range(group)], axis=0)
    cross = jnp.concatenate([rest[p, rows:] for p in range(group)], axis=0)
    inverse = inverse[...]
    mixed = product(cross, inverse, NT)
    change = refine(off[...] + lost, turned[...], inverse)
    whole = inverse + product(change, inverse, NN)
    mixed = mixed + close_product(mixed, change, NT)
    coupling_held[...] = mixed
    left = left_terms(jnp.concatenate([whole * scale, product(mixed, whole, NN)], axis=0))

    def store(src, dst, place):
        pltpu.make_async_copy(src, dst, store_sem.at[place]).start()

    store(coupling_held, coupling, 2)
    for i in range(steps):
        span, at = slice(i * chunk, (i + 1) * chunk), pl.ds(i * chunk, chunk)
        one, two, three = (pieces[t * size : (t + 1) * size, span] for t in range(3))
        out = dot(left, jnp.concatenate([one, three, two, one, two, one], axis=0), NN)
        basis_held[:, span] = out[:size]
        store(basis_held.at[:, at], basis.at[:, at], 0)
        updated_held[:, span] = trailing[:, span] - out[size:]
        store(updated_held.at[:, at], updated.at[:, at], 1)
    row = lax.broadcasted_iota(jnp.int32, (size, size), 0)
    lane = lax.broadcasted_iota(jnp.int32, (size, size), 1)
    total = product(whole, gram[...], NN) + dot(whole.astype(jnp.bfloat16), lost.astype(jnp.bfloat16), NN)
    upper_held[...] = jnp.where(row <= lane, total * (1.0 / scale), 0.0)
    store(upper_held, upper, 3)
    for place, (src, dst) in enumerate(((basis_held, basis), (updated_held, updated), (coupling_held, coupling), (upper_held, upper))):
        pltpu.make_async_copy(src, dst, store_sem.at[place]).wait()


def shards(sizes, panel, trailing):
    size, width = panel.shape
    trail = trailing.shape[0]
    nx, ny, nz = sizes
    group = nx * ny
    rows, less = size // group, trail // group
    f32 = jnp.float32
    scale = float(width * group * nz) ** 0.5

    def params(identity=None, mebibytes=40):
        return pltpu.CompilerParams(
            collective_id=identity, has_side_effects=identity is not None, vmem_limit_bytes=mebibytes * 2**20
        )

    square = jax.ShapeDtypeStruct((size, size), f32)
    held = pl.pallas_call(
        functools.partial(reduce_kernel, sizes),
        out_shape=[
            square,
            jax.ShapeDtypeStruct((group, rows + less, size), f32),
            square,
            square,
            square,
            jax.ShapeDtypeStruct((3 * size, width), jnp.bfloat16),
            jax.ShapeDtypeStruct((trail, width), f32),
        ],
        in_specs=[HBM, HBM],
        out_specs=[VMEM] * 7,
        scratch_shapes=[
            pltpu.VMEM((size, width), f32),
            pltpu.SemaphoreType.DMA((len(spans_of(width)) + 1,)),
            *exchange_scratch(sizes, rows, size),
            *exchange_scratch(sizes, rows + less, size),
            *[pltpu.VMEM((1, 2 * size, span.stop - span.start), jnp.bfloat16) for span in spans_of(width)],
        ],
        compiler_params=params(0),
        name="reduce",
    )(pltpu.with_memory_space_constraint(panel, pltpu.HBM), pltpu.with_memory_space_constraint(trailing, pltpu.HBM))
    basis, upper, coupling_t, updated = pl.pallas_call(
        functools.partial(final_kernel, scale),
        out_shape=[
            jax.ShapeDtypeStruct((size, width), f32),
            square,
            jax.ShapeDtypeStruct((trail, size), f32),
            jax.ShapeDtypeStruct((trail, width), f32),
        ],
        in_specs=[VMEM] * 7,
        out_specs=[HBM] * 4,
        scratch_shapes=[
            pltpu.VMEM((size, width), f32),
            pltpu.VMEM((trail, width), f32),
            pltpu.VMEM((size, size), f32),
            pltpu.VMEM((trail, size), f32),
            pltpu.SemaphoreType.DMA((4,)),
        ],
        compiler_params=params(),
        name="final",
    )(*held)
    return basis, upper, coupling_t.T, updated


def solution(mesh):
    sizes = tuple(mesh.shape[name] for name in ("gx", "gy", "gz"))
    placed = P(None, ("gx", "gy", "gz"))
    return jax.shard_map(
        functools.partial(shards, sizes),
        mesh=mesh,
        in_specs=(placed, placed),
        out_specs=(placed, P(), P(), placed),
        check_vma=False,
    )
```
